512 devices in a mesh: docs: 16 (over y, x), supp: 32 (over z, core).
Axes of the slice: x: 4, y: 4, z: 16, core: 2. Of those that a mesh axis runs over, the one named last changes fastest.
Arguments:
- vocab_table: bfloat16 [100000, 300], P('docs'), may hold values from -0.69140625 to 0.69140625
- support_atoms: bfloat16 [65536, 300], P('supp'), may hold values from -0.69140625 to 0.69140625
- weight_logits: float32 [65536], P('supp'), may hold values from -6 to 6
- word_counts: int32 [32], P('docs'), may hold values from 1 to 600, 11520 in all
- word_shard: int32 [20480, 1], P('docs'), may hold values from 0 to 15; in each aligned block of 1280 rows (0 to 1279, 1280 to 2559, ...) at most 128 rows name the same one
- word_row: int32 [20480], P('docs'), may hold values from 0 to 6249
Outputs:
- row_potential: float32 [32, 640], P('docs')
- col_potential: float32 [32, 65536], P('docs', 'supp')
- new_log_weights: float32 [65536], P('supp')
The draws below stay inside these ranges and needn't reach their ends.
Inputs may be any that keep to these rules, and one draw needn't show every extreme that they name: `word_shard`: within the 1280 word slots of each index of docs (aligned blocks), no shard number appears more than 128 times, and some number appears exactly 128 times. `word_counts`: the longest document has exactly 600 words.
All inputs are finite; a program needn't handle non-finite values. No bound on the sum of `word_counts` on one device may be relied on, other than what follows from the above.
Results may differ from the reference program's by a relative error of at most 0.0003.
Values may be sent and summed in bfloat16 or wider, within the bound.
No kernel may reach another device: no remote copies, remote signals or barrier semaphores. Data moves between devices by JAX's collectives and lax.ppermute only.
A program may use at most 64 MiB of HBM per device.

```python
import math
import jax
import jax.numpy as jnp
import numpy as np
from jax import lax

D = 300
VOC_DEV = 6250
VOCAB = 100000
NS = 65536
DOC_DEV = 2
NDOC = 32
LMAX = 640
LONGEST = 600
ITERS = 2
CAP = 128
N_DOCS = 16


def touch_ends(result, own_key, low, top_value):
    longest = result.shape.index(max(result.shape))
    spots = []
    for shift in (0, 1):
        where = [jax.random.randint(jax.random.fold_in(own_key, axis), (), 0, length) for axis, length in enumerate(result.shape)]
        where[longest] = (where[longest] + shift) % result.shape[longest]
        spots.append(tuple(where))
    return result.at[spots[0]].set(low).at[spots[1]].set(top_value)


def block_scale(key, shape, pieces, least, high):
    level = 1.0
    for axis_at, blocks in pieces:
        steps = jax.random.uniform(jax.random.fold_in(jax.random.fold_in(key, 6), axis_at), (blocks,), jnp.float32, least / len(pieces), high / len(pieces))
        level = level * jnp.repeat(jnp.exp(steps), shape[axis_at] // blocks).reshape((-1,) + (1,) * (len(shape) - 1 - axis_at))
    return level


def profile(count, total, reach, skew):
    weights = [(1 << 20) // math.isqrt(standing ** skew) + 1 for standing in range(2, count + 1)]
    spare, given = total - reach - (count - 1), [1] * (count - 1)
    while spare > 0:
        movable = [i for i in range(count - 1) if given[i] < reach]
        whole, budget = sum([weights[i] for i in movable]), spare
        for i in movable:
            addition = min(reach - given[i], max(1, budget * weights[i] // whole), spare)
            given[i] = given[i] + addition
            spare = spare - addition
    return np.array([reach] + given)


def ragged(key, number_of, total, most, skew):
    if number_of == 2:
        one = jax.random.randint(key, (), max(1, total - most), min(most, total - 1) + 1)
        return jnp.stack([one, total - one])
    tallies = jnp.asarray(profile(number_of, total, most, skew), jnp.int32)
    couples = (number_of - 1) // 2
    donor, sink = tallies[1:1 + 2 * couples:2], tallies[2:2 + 2 * couples:2]
    margin = jnp.minimum(donor - 1, most - sink)
    passed = jax.random.randint(jax.random.fold_in(key, 1), (couples,), 0, 1 << 20) % (margin + 1)
    tallies = tallies.at[1:1 + 2 * couples:2].set(donor - passed).at[2:2 + 2 * couples:2].set(sink + passed)
    return tallies[jax.random.permutation(jax.random.fold_in(key, 2), number_of)]


def shared_out(key, own, number, rows, number_of, top, reach, slope):
    ranking = jax.random.permutation(key, number_of)
    packed, usual = shares(number_of, rows * top, reach, slope, True), shares(number_of, rows * top, reach, slope, False)
    places = jnp.arange(number_of)

    def named(lengths, rotation):
        used = int((lengths > 0).sum())
        fixed = max(1, used // 4)
        moved = fixed + (places - fixed + rotation * (used - fixed)) % max(1, number_of - fixed)
        return jnp.zeros((number_of,), jnp.int32).at[ranking[jnp.where(places < fixed, places, moved)]].set(jnp.asarray(lengths, jnp.int32))

    lengths = jnp.where(number % 4 == 0, named(packed, number // 4), named(usual, number - number // 4 - 1))
    mixed = jax.random.permutation(jax.random.fold_in(own, 3), number_of)
    source_of, taker = mixed[0:number_of // 2 * 2:2], mixed[1:number_of // 2 * 2:2]
    slack = jnp.minimum(lengths[source_of] - 1, reach - lengths[taker]) // 2
    slack = jnp.where((source_of == ranking[0]) | (taker == ranking[0]) | (lengths[taker] == 0), 0, jnp.maximum(slack, 0))
    moved = jax.random.randint(jax.random.fold_in(own, 4), (number_of // 2,), 0, 1 << 20) % (slack + 1)
    lengths = lengths.at[source_of].add(-moved).at[taker].add(moved)
    items = jnp.searchsorted(jnp.cumsum(lengths), jnp.arange(rows * top), side="right").astype(jnp.int32)
    grid = items.reshape(top, rows).T
    grid = grid[jax.random.permutation(jax.random.fold_in(own, 1), rows)]
    rotation = jax.random.randint(jax.random.fold_in(own, 2), (rows, 1), 0, top)
    return jnp.take_along_axis(grid, (jnp.arange(top)[None, :] + rotation) % top, axis=1)


def shares(amount, total, reach, skew, full):
    weights = [(1 << 20) // math.isqrt(grade ** skew) + 1 for grade in range(1, amount + 1)]
    largest = reach if full else min(reach, max(-(-total // amount), total * weights[0] // sum(weights)))
    least = 1 if total - largest >= amount - 1 else 0
    counts, spare = [largest] + [least] * (amount - 1), total - largest - least * (amount - 1)
    while spare > 0:
        free = [i for i in range(1, amount) if counts[i] < largest] or [i for i in range(1, amount) if counts[i] < reach]
        pool, remaining = sum([weights[i] for i in free]), spare
        for i in free:
            more = min(reach - counts[i], max(1, remaining * weights[i] // pool), spare)
            counts[i] = counts[i] + more
            spare = spare - more
    return np.array(counts)


def scatter_about(own_key, shape, scale, limit, shards=(), dtype=jnp.bfloat16):
    drawn = scale * jax.random.normal(own_key, shape, jnp.float32)
    if shards:
        drawn = drawn * block_scale(own_key, shape, shards, -0.22, 0.18)
    return jnp.clip(drawn, -limit, limit).astype(dtype)


def setup_inputs(seed: int = 0) -> dict:
    seeds = jax.random.split(jax.random.key(seed), 7)
    vocab_table = scatter_about(seeds[0], (VOCAB, D), (2.0 / D ** 0.5), 0.69140625, ((0, 16),))
    support_atoms = scatter_about(seeds[1], (NS, D), (2.0 / D ** 0.5), 0.69140625, ((0, 32),))
    weight_logits = scatter_about(seeds[2], (NS,), 1.0, 6.0, ((0, 32),), jnp.float32)
    word_counts = ragged(seeds[3], NDOC, NDOC * LONGEST * 3 // 5, LONGEST, 2).astype(jnp.int32)
    word_shard_keys = jax.random.split(jax.random.fold_in(seeds[4], 1), (NDOC * LMAX) // (DOC_DEV * LMAX))
    word_shard_turns = jax.random.permutation(jax.random.fold_in(seeds[4], 3), (NDOC * LMAX) // (DOC_DEV * LMAX))
    word_shard = jax.vmap(lambda own, number: shared_out(jax.random.fold_in(seeds[4], 2), own, number, DOC_DEV * LMAX, N_DOCS, 1, CAP, 2))(word_shard_keys, word_shard_turns).reshape((NDOC * LMAX, 1))
    word_row = touch_ends(jax.random.randint(seeds[5], (NDOC * LMAX,), 0, VOC_DEV), jax.random.fold_in(seeds[5], 1), 0, VOC_DEV - 1).astype(jnp.int32)
    return dict(vocab_table=vocab_table, support_atoms=support_atoms, weight_logits=weight_logits, word_counts=word_counts, word_shard=word_shard, word_row=word_row)


epsilon = 0.05


def extent(values, axis):
    largest = jnp.max(values, axis=axis, keepdims=True)
    return largest + jnp.log(jnp.sum(jnp.exp(values - largest), axis=axis, keepdims=True))


def reference(vocab_table, support_atoms, weight_logits, word_counts, word_shard, word_row):
    vocab_index = word_shard[:, 0] * VOC_DEV + word_row
    word_vecs = vocab_table[vocab_index].reshape(NDOC, LMAX, D)
    atoms_sq = jnp.sum(jnp.square(support_atoms.astype(jnp.float32)), axis=1)
    log_base = weight_logits - extent(weight_logits, 0)
    positions = jnp.arange(LMAX)

    def one_doc(inputs):
        doc_words, word_count = inputs
        words_sq = jnp.sum(jnp.square(doc_words.astype(jnp.float32)), axis=1)
        product = jnp.dot(doc_words, support_atoms.T, preferred_element_type=jnp.float32)
        dist_grid = words_sq[:, None] + atoms_sq[None, :] - 2.0 * product
        live_mask = positions < word_count

        def column_extent(row_pot):
            scores = (row_pot[:, None] - dist_grid) / epsilon
            largest = jnp.max(jnp.where(live_mask[:, None], scores, -jnp.inf), axis=0)
            summed = jnp.sum(jnp.where(live_mask[:, None], jnp.exp(scores - largest[None, :]), 0.0), axis=0)
            return largest + jnp.log(summed)

        row_pot = jnp.zeros((LMAX,), jnp.float32)
        log_share = -epsilon * jnp.log(word_count.astype(jnp.float32))
        col_pot = jnp.zeros((NS,), jnp.float32)
        for sweep in range(ITERS):
            col_pot = epsilon * log_base - epsilon * column_extent(row_pot)
            scores = (col_pot[None, :] - dist_grid) / epsilon
            row_ext = extent(scores, 1)[:, 0]
            row_pot = jnp.where(live_mask, log_share - epsilon * row_ext, 0.0)
        log_marg = col_pot / epsilon + column_extent(row_pot)
        return row_pot, col_pot, log_marg

    row_pot, col_pot, log_marg = lax.map(one_doc, (word_vecs, word_counts))
    mean_log = jnp.sum(log_marg, axis=0) / NDOC
    new_log = mean_log - extent(mean_log, 0)
    return row_pot, col_pot, new_log
```

```python
import jax
import jax.numpy as jnp
from jax import lax
from jax.experimental import pallas as pl
from jax.experimental.pallas import tpu as pltpu
from jax.sharding import PartitionSpec as P

EPS = 0.05
LOG2E = 1.4426950408889634
LN2 = 0.6931471805599453
CAP = 128
HALF = CAP // 2
LANES = 128
FAR = 1e30
VMEM = pl.BlockSpec(memory_space=pltpu.VMEM)
SMEM = pl.BlockSpec(memory_space=pltpu.SMEM)
NT = (((1,), (1,)), ((), ()))


def call(kernel, out_shape, in_specs, scratch=(), limit=24):
    return pl.pallas_call(
        kernel,
        out_shape=out_shape,
        in_specs=in_specs,
        out_specs=jax.tree.map(lambda _: VMEM, out_shape),
        scratch_shapes=list(scratch),
        compiler_params=pltpu.CompilerParams(vmem_limit_bytes=limit << 20),
    )


def f32(shape):
    return jax.ShapeDtypeStruct(shape, jnp.float32)


def eye_mask():
    rows = lax.broadcasted_iota(jnp.int32, (LANES, LANES), 0)
    cols = lax.broadcasted_iota(jnp.int32, (LANES, LANES), 1)
    return rows == cols


def rowify(column, eye):
    return jnp.sum(jnp.where(eye, column, 0.0), axis=0, keepdims=True)


def colify(row, eye):
    return jnp.sum(jnp.where(eye, row, 0.0), axis=1, keepdims=True)


def request_kernel(core_ref, shard_ref, row_ref, req_ref, pos_ref):
    groups = req_ref.shape[0]
    slots = shard_ref.shape[1]
    core = core_ref[0]
    tri = (
        lax.broadcasted_iota(jnp.int32, (LANES, LANES), 0)
        <= lax.broadcasted_iota(jnp.int32, (LANES, LANES), 1)
    ).astype(jnp.bfloat16)
    owner_ids = lax.broadcasted_iota(jnp.int32, (groups, LANES), 0)
    seats = lax.broadcasted_iota(jnp.int32, (HALF, LANES), 0) + core * HALF
    seen = jnp.zeros((groups, 1), jnp.float32)
    req = jnp.zeros((2 * groups, HALF), jnp.float32)
    for block in range(slots // LANES):
        span = slice(block * LANES, (block + 1) * LANES)
        shard = shard_ref[:, span]
        row = row_ref[:, span]
        member = (owner_ids == shard).astype(jnp.float32)
        counted = seen + jnp.dot(member.astype(jnp.bfloat16), tri, preferred_element_type=jnp.float32)
        seen = counted[:, LANES - 1 :]
        rank = jnp.sum(member * (counted - 1.0), axis=0, keepdims=True).astype(jnp.int32)
        seated = (seats == rank).astype(jnp.float32).astype(jnp.bfloat16)
        high = member * (row >> 7).astype(jnp.float32)
        low = member * (row & 127).astype(jnp.float32)
        both = jnp.concatenate([high, low], axis=0).astype(jnp.bfloat16)
        req += lax.dot_general(both, seated, NT, preferred_element_type=jnp.float32)
        side = (rank >> 6) ^ core
        pos_ref[:, span] = side * (groups * HALF) + shard * HALF + (rank & (HALF - 1))
    req_ref[...] = (req[:groups] * 128.0 + req[groups:]).astype(jnp.int32)


def first_kernel(
    count_ref, own_ref, other_ref, pos_ref, atom_ref, logit_ref,
    plan_ref, sent_ref, peak_ref, start_ref,
    score_ref, head_ref, peak_col, mass_col,
):
    docs, atoms = start_ref.shape
    slots = plan_ref.shape[0]
    doc_slots = slots // docs
    half_rows = own_ref.shape[0]
    wide = min(512, atoms)
    for doc in range(docs):
        base = doc * doc_slots

        def score_step(step, top):
            at = pl.multiple_of(base + step * LANES, LANES)
            place = pos_ref[pl.ds(at, LANES), :]
            seats = lax.broadcasted_iota(jnp.int32, (LANES, half_rows), 1)
            own_hot = (seats == place).astype(jnp.float32).astype(jnp.bfloat16)
            other_hot = (seats + half_rows == place).astype(jnp.float32).astype(jnp.bfloat16)
            words = jnp.dot(own_hot, own_ref[...], preferred_element_type=jnp.float32)
            words += jnp.dot(other_hot, other_ref[...], preferred_element_type=jnp.float32)
            square = jnp.sum(words * words, axis=1, keepdims=True) * (LOG2E / EPS)
            slot = step * LANES + lax.broadcasted_iota(jnp.int32, (LANES, 1), 0)
            square = jnp.where(slot < count_ref[doc], square, FAR)
            words = words.astype(jnp.bfloat16)
            tops = []
            for left in range(0, atoms, wide):
                product = lax.dot_general(
                    words, atom_ref[left : left + wide, :], NT, preferred_element_type=jnp.float32
                )
                score = product * (2.0 * LOG2E / EPS) - square
                score_ref[pl.ds(at, LANES), left : left + wide] = score
                tops.append(jnp.max(score.reshape(LANES // 8, 8, wide), axis=0))
            return jnp.maximum(top, jnp.concatenate(tops, axis=1))

        top = lax.fori_loop(
            0, doc_slots // LANES, score_step, jnp.full((8, atoms), -jnp.inf, jnp.float32)
        )
        top = jnp.max(top, axis=0, keepdims=True)
        head_ref[...] = jnp.broadcast_to(top, (8, atoms))

        def sum_step(step, total):
            at = pl.multiple_of(base + step * 32, 32)
            for part in range(4):
                total += jnp.exp2(score_ref[pl.ds(at + part * 8, 8), :] - head_ref[...])
            return total

        total = lax.fori_loop(0, doc_slots // 32, sum_step, jnp.zeros((8, atoms), jnp.float32))
        total = jnp.sum(total, axis=0, keepdims=True)
        head = logit_ref[...] * LOG2E - top - jnp.log(total) * LOG2E
        start_ref[doc : doc + 1, :] = head
        head_ref[...] = jnp.broadcast_to(head, (8, atoms))

        def plan_step(step, carry):
            at = pl.multiple_of(base + step * 16, 16)
            upper = score_ref[pl.ds(at, 8), :] + head_ref[...]
            lower = score_ref[pl.ds(at + 8, 8), :] + head_ref[...]
            score = jnp.concatenate([upper, lower], axis=0)
            peak = jnp.max(score, axis=1, keepdims=True)
            share = jnp.exp2(score - peak)
            plan_ref[pl.ds(at, 16), :] = share.astype(plan_ref.dtype)
            peak_col[pl.ds(at, 16), :] = peak
            mass_col[pl.ds(at, 16), :] = jnp.sum(share, axis=1, keepdims=True)
            return carry

        lax.fori_loop(0, doc_slots // 16, plan_step, 0)

    eye = eye_mask()
    copies = sent_ref.shape[0]
    for block in range(slots // LANES):
        span = slice(block * LANES, (block + 1) * LANES)
        peak = rowify(peak_col[span, :], eye)
        mass = rowify(mass_col[span, :], eye)
        peak_ref[:, span] = peak
        extent = peak + jnp.log(mass) * LOG2E
        for copy in range(copies):
            sent_ref[copy, :, span] = extent
    logits = logit_ref[...] * LOG2E
    top = jnp.max(logits, axis=1, keepdims=True)
    whole = top + jnp.log(jnp.sum(jnp.exp2(logits - top), axis=1, keepdims=True)) * LOG2E
    for copy in range(copies):
        sent_ref[copy, :, slots:] = jnp.broadcast_to(whole, (1, LANES))


def slot_rows(count_ref, docs, slots):
    doc_slots = slots // docs
    lane = lax.broadcasted_iota(jnp.int32, (1, slots), 1)
    words = jnp.full((1, slots), count_ref[0], jnp.int32)
    first = jnp.zeros((1, slots), jnp.int32)
    for doc in range(1, docs):
        inside = lane >= doc * doc_slots
        words = jnp.where(inside, count_ref[doc], words)
        first = jnp.where(inside, doc * doc_slots, first)
    live = lane - first < words
    words = words.astype(jnp.float32)
    return live, words


def column_sums(plan_ref, weight_col, base, doc_slots):
    atoms = plan_ref.shape[1]

    def step_sum(step, total):
        at = pl.multiple_of(base + step * 16, 16)
        part = plan_ref[pl.ds(at, 16), :].astype(jnp.float32) * weight_col[pl.ds(at, 16), :]
        return total + part[:8] + part[8:]

    total = lax.fori_loop(0, doc_slots // 16, step_sum, jnp.zeros((8, atoms), jnp.float32))
    return jnp.sum(total, axis=0, keepdims=True)


def second_kernel(
    count_ref, got_ref, peak_ref, plan_ref, start_ref, logit_ref, square_ref,
    sent_ref, scale_ref, base_ref, gain_ref, col_ref,
    scale_col, mass_col, head_ref,
):
    docs, atoms = start_ref.shape
    slots = plan_ref.shape[0]
    doc_slots = slots // docs
    copies = got_ref.shape[0]
    top = got_ref[0]
    for copy in range(1, copies):
        top = jnp.maximum(top, got_ref[copy])
    mass = jnp.zeros_like(top)
    for copy in range(copies):
        mass += jnp.exp2(got_ref[copy] - top)
    extent = top + jnp.log(mass) * LOG2E
    whole = extent[:, slots : slots + 1]
    extent = extent[:, :slots]
    live, words = slot_rows(count_ref, docs, slots)
    scale = jnp.where(live, jnp.exp2(peak_ref[...] - extent) / words, 0.0)
    scale_ref[...] = scale
    base_ref[...] = (2.0 * EPS * LN2) * whole - EPS * jnp.log(words) - (EPS * LN2) * extent
    eye = eye_mask()
    for block in range(slots // LANES):
        span = slice(block * LANES, (block + 1) * LANES)
        scale_col[span, :] = colify(scale[:, span], eye)
    for doc in range(docs):
        base = doc * doc_slots
        total = column_sums(plan_ref, scale_col, base, doc_slots)
        gain_log = logit_ref[...] - jnp.log(total)
        gain = jnp.exp(gain_log)
        gain_ref[doc : doc + 1, :] = gain_log
        col_ref[doc : doc + 1, :] = (
            EPS * (LN2 * start_ref[doc : doc + 1, :] + gain_log)
            + square_ref[...]
            - (2.0 * EPS * LN2) * whole
        )
        head_ref[...] = jnp.broadcast_to(gain, (8, atoms))

        def row_step(step, carry):
            at = pl.multiple_of(base + step * 16, 16)
            part = plan_ref[pl.ds(at, 16), :].astype(jnp.float32)
            upper = jnp.sum(part[:8] * head_ref[...], axis=1, keepdims=True)
            lower = jnp.sum(part[8:] * head_ref[...], axis=1, keepdims=True)
            mass_col[pl.ds(at, 8), :] = upper
            mass_col[pl.ds(at + 8, 8), :] = lower
            return carry

        lax.fori_loop(0, doc_slots // 16, row_step, 0)
    for block in range(slots // LANES):
        span = slice(block * LANES, (block + 1) * LANES)
        part = rowify(mass_col[span, :], eye) * scale[:, span]
        for copy in range(copies):
            sent_ref[copy, :, span] = part


def third_kernel(
    count_ref, got_ref, scale_ref, base_ref, plan_ref, gain_ref,
    sent_ref, row_ref,
    scale_col,
):
    docs, atoms = gain_ref.shape
    slots = plan_ref.shape[0]
    doc_slots = slots // docs
    mass = got_ref[0]
    for copy in range(1, got_ref.shape[0]):
        mass += got_ref[copy]
    live, words = slot_rows(count_ref, docs, slots)
    mass = jnp.where(live, mass, 1.0) * words
    row_ref[...] = jnp.where(live, base_ref[...] - EPS * jnp.log(mass), 0.0)
    scale = scale_ref[...] / mass
    eye = eye_mask()
    for block in range(slots // LANES):
        span = slice(block * LANES, (block + 1) * LANES)
        scale_col[span, :] = colify(scale[:, span], eye)
    marginal = jnp.zeros((1, atoms), jnp.float32)
    for doc in range(docs):
        total = column_sums(plan_ref, scale_col, doc * doc_slots, doc_slots)
        marginal += gain_ref[doc : doc + 1, :] + jnp.log(total)
    for copy in range(sent_ref.shape[0]):
        sent_ref[copy] = marginal


def mean_kernel(documents, got_ref, mean_ref, sent_ref):
    total = got_ref[0]
    for copy in range(1, got_ref.shape[0]):
        total += got_ref[copy]
    mean = total * (1.0 / documents)
    mean_ref[...] = mean
    top = jnp.max(mean, axis=1, keepdims=True)
    extent = top + jnp.log(jnp.sum(jnp.exp(mean - top), axis=1, keepdims=True))
    for copy in range(sent_ref.shape[0]):
        sent_ref[copy] = jnp.broadcast_to(extent, (1, LANES))


def final_kernel(got_ref, mean_ref, new_ref):
    top = got_ref[0]
    for copy in range(1, got_ref.shape[0]):
        top = jnp.maximum(top, got_ref[copy])
    mass = jnp.zeros_like(top)
    for copy in range(got_ref.shape[0]):
        mass += jnp.exp(got_ref[copy] - top)
    extent = top + jnp.log(mass)
    new_ref[...] = mean_ref[...] - extent[:, :1]


def swap(x, axis):
    return lax.all_to_all(x, axis, split_axis=0, concat_axis=0, tiled=True)


def shards(vocab_table, support_atoms, weight_logits, word_counts, word_shard, word_row):
    groups = lax.axis_size("docs")
    parts = lax.axis_size("supp")
    docs = word_counts.shape[0]
    slots = word_row.shape[0]
    atoms, width = support_atoms.shape
    core = (lax.axis_index("supp") & 1).astype(jnp.int32).reshape(1)

    requests, place = call(
        request_kernel,
        (
            jax.ShapeDtypeStruct((groups, HALF), jnp.int32),
            jax.ShapeDtypeStruct((1, slots), jnp.int32),
        ),
        [SMEM, VMEM, VMEM],
        limit=8,
    )(core, word_shard.reshape(1, slots), word_row.reshape(1, slots))
    asked = swap(requests.reshape(groups, 1, HALF), "docs")
    found = vocab_table[asked.reshape(groups * HALF)]
    own = swap(found.reshape(groups, HALF, width), "docs").reshape(groups * HALF, width)
    other = lax.ppermute(own, "supp", [(i, i ^ 1) for i in range(parts)])

    logits = weight_logits.reshape(1, atoms)
    square = jnp.sum(jnp.square(support_atoms.astype(jnp.float32)), axis=1).reshape(1, atoms)
    plan, extent, peak, start = call(
        first_kernel,
        (
            jax.ShapeDtypeStruct((slots, atoms), jnp.bfloat16),
            f32((parts, 1, slots + LANES)),
            f32((1, slots)),
            f32((docs, atoms)),
        ),
        [SMEM, VMEM, VMEM, VMEM, VMEM, VMEM],
        [
            pltpu.VMEM((slots, atoms), jnp.float32),
            pltpu.VMEM((8, atoms), jnp.float32),
            pltpu.VMEM((slots, 1), jnp.float32),
            pltpu.VMEM((slots, 1), jnp.float32),
        ],
        limit=40,
    )(word_counts, own, other, place.reshape(slots, 1), support_atoms, logits)
    extents = swap(extent, "supp")
    mass, scale, base, gain, col_pot = call(
        second_kernel,
        (
            f32((parts, 1, slots)),
            f32((1, slots)),
            f32((1, slots)),
            f32((docs, atoms)),
            f32((docs, atoms)),
        ),
        [SMEM, VMEM, VMEM, VMEM, VMEM, VMEM, VMEM],
        [
            pltpu.VMEM((slots, 1), jnp.float32),
            pltpu.VMEM((slots, 1), jnp.float32),
            pltpu.VMEM((8, atoms), jnp.float32),
        ],
    )(word_counts, extents, peak, plan, start, logits, square)
    masses = swap(mass, "supp")
    marginal, row_pot = call(
        third_kernel,
        (f32((groups, 1, atoms)), f32((1, slots))),
        [SMEM, VMEM, VMEM, VMEM, VMEM, VMEM],
        [pltpu.VMEM((slots, 1), jnp.float32)],
    )(word_counts, masses, scale, base, plan, gain)
    marginals = swap(marginal, "docs")
    mean, part = call(
        lambda *refs: mean_kernel(docs * groups, *refs),
        (f32((1, atoms)), f32((parts, 1, LANES))),
        [VMEM],
    )(marginals)
    new_log = call(final_kernel, f32((1, atoms)), [VMEM, VMEM])(swap(part, "supp"), mean)
    return row_pot.reshape(docs, slots // docs), col_pot, new_log.reshape(atoms)


def solution(mesh):
    placed = (P("docs", None), P("supp", None), P("supp"), P("docs"), P("docs", None), P("docs"))
    return jax.shard_map(
        shards,
        mesh=mesh,
        in_specs=placed,
        out_specs=(P("docs", None), P("docs", "supp"), P("supp")),
        check_vma=False,
    )
```

```python
import jax
import jax.numpy as jnp
from jax import lax
from jax.experimental import pallas as pl
from jax.experimental.pallas import tpu as pltpu
from jax.sharding import PartitionSpec as P

EPS = 0.05
LOG2E = 1.4426950408889634
LN2 = 0.6931471805599453
CAP = 128
HALF = CAP // 2
LANES = 128
FAR = 1e30
WIDE = 256
VMEM = pl.BlockSpec(memory_space=pltpu.VMEM)
SMEM = pl.BlockSpec(memory_space=pltpu.SMEM)
NT = (((1,), (1,)), ((), ()))


def call(kernel, out_shape, in_specs, scratch=(), limit=24):
    return pl.pallas_call(
        kernel,
        out_shape=out_shape,
        in_specs=in_specs,
        out_specs=jax.tree.map(lambda _: VMEM, out_shape),
        scratch_shapes=list(scratch),
        compiler_params=pltpu.CompilerParams(vmem_limit_bytes=limit << 20),
    )


def f32(shape):
    return jax.ShapeDtypeStruct(shape, jnp.float32)


def eye_mask():
    rows = lax.broadcasted_iota(jnp.int32, (LANES, LANES), 0)
    cols = lax.broadcasted_iota(jnp.int32, (LANES, LANES), 1)
    return rows == cols


def rowify(column, eye):
    return jnp.sum(jnp.where(eye, column, 0.0), axis=0, keepdims=True)


def colify(row, eye):
    return jnp.sum(jnp.where(eye, row, 0.0), axis=1, keepdims=True)


def request_kernel(core_ref, shard_ref, row_ref, req_ref, pos_ref):
    groups = req_ref.shape[0]
    slots = shard_ref.shape[1]
    doc_slots = pos_ref.shape[1]
    core = core_ref[0]
    tri = (
        lax.broadcasted_iota(jnp.int32, (LANES, LANES), 0)
        <= lax.broadcasted_iota(jnp.int32, (LANES, LANES), 1)
    ).astype(jnp.bfloat16)
    owner_ids = lax.broadcasted_iota(jnp.int32, (groups, LANES), 0)
    seats = lax.broadcasted_iota(jnp.int32, (HALF, LANES), 0) + core * HALF
    seen = jnp.zeros((groups, 1), jnp.float32)
    req = jnp.zeros((2 * groups, HALF), jnp.float32)
    places = []
    for block in range(slots // LANES):
        span = slice(block * LANES, (block + 1) * LANES)
        shard = shard_ref[:, span]
        row = row_ref[:, span]
        member = (owner_ids == shard).astype(jnp.float32)
        counted = seen + jnp.dot(member.astype(jnp.bfloat16), tri, preferred_element_type=jnp.float32)
        seen = counted[:, LANES - 1 :]
        rank = jnp.sum(member * (counted - 1.0), axis=0, keepdims=True).astype(jnp.int32)
        seated = (seats == rank).astype(jnp.float32).astype(jnp.bfloat16)
        high = member * (row >> 7).astype(jnp.float32)
        low = member * (row & 127).astype(jnp.float32)
        both = jnp.concatenate([high, low], axis=0).astype(jnp.bfloat16)
        req += lax.dot_general(both, seated, NT, preferred_element_type=jnp.float32)
        side = (rank >> 6) ^ core
        places.append(side * (groups * HALF) + shard * HALF + (rank & (HALF - 1)))
    req_ref[...] = (req[:groups] * 128.0 + req[groups:]).astype(jnp.int32)
    own_blocks = doc_slots // LANES
    for block in range(own_blocks):
        span = slice(block * LANES, (block + 1) * LANES)
        pos_ref[:, span] = jnp.where(core == 0, places[block], places[own_blocks + block])


def own_count(core_ref, count_ref):
    return jnp.where(core_ref[0] == 0, count_ref[0], count_ref[1])


def first_kernel(
    core_ref, count_ref, own_ref, other_ref, pos_ref,
    own_atom_ref, other_atom_ref, own_logit_ref, other_logit_ref,
    plan_ref, sent_ref, peak_ref, start_ref,
    hot_ref, word_ref, square_ref, score_refs, far_refs, head_ref, near_ref, mass_ref,
):
    slots, all_atoms = plan_ref.shape
    half_rows = own_ref.shape[0]
    quarters = len(score_refs)
    quarter = all_atoms // quarters
    blocks = slots // LANES
    count = own_count(core_ref, count_ref)
    eye = eye_mask()
    seats = lax.broadcasted_iota(jnp.int32, (LANES, 2 * half_rows), 1).astype(jnp.float32)
    for block in range(blocks):
        span = slice(block * LANES, (block + 1) * LANES)
        place = colify(pos_ref[:, span].astype(jnp.float32), eye)
        hot_ref[span, :] = (seats == place).astype(jnp.float32).astype(jnp.bfloat16)
    words = jnp.dot(hot_ref[:, :half_rows], own_ref[...], preferred_element_type=jnp.float32)
    words += jnp.dot(hot_ref[:, half_rows:], other_ref[...], preferred_element_type=jnp.float32)
    square = jnp.sum(words * words, axis=1, keepdims=True) * (LOG2E / EPS)
    slot = lax.broadcasted_iota(jnp.int32, (slots, 1), 0)
    square = jnp.where(slot < count, square, FAR)
    square_ref[...] = jnp.broadcast_to(square, (slots, LANES))
    word_ref[...] = words.astype(jnp.bfloat16)
    for far_ref in far_refs:
        far_ref[...] = jnp.full(far_ref.shape, -jnp.inf, jnp.float32)

    def score_step(step, carry):
        at = pl.multiple_of(step * WIDE, WIDE)
        for part in range(quarters):
            half, inner = divmod(part, quarters // 2)
            atom_ref = (own_atom_ref, other_atom_ref)[half]
            logit_ref = (own_logit_ref, other_logit_ref)[half]
            score_ref, far_ref = score_refs[part], far_refs[part]
            source = pl.ds(pl.multiple_of(inner * quarter + at, WIDE), WIDE)
            product = jnp.dot(word_ref[...], atom_ref[:, source], preferred_element_type=jnp.float32)
            tiles = [
                product[:, left : left + LANES] * (2.0 * LOG2E / EPS) - square_ref[...]
                for left in range(0, WIDE, LANES)
            ]
            for tile, score in enumerate(tiles):
                score_ref[:, pl.ds(at + tile * LANES, LANES)] = score
            score = score_ref[:, pl.ds(at, WIDE)]
            top = jnp.max(score, axis=0, keepdims=True)
            total = jnp.sum(jnp.exp2(score - top), axis=0, keepdims=True)
            head = logit_ref[:, source] * LOG2E - top - jnp.log(total) * LOG2E
            start_ref[:, pl.ds(pl.multiple_of(part * quarter + at, WIDE), WIDE)] = head
            far = far_ref[...]
            for left in range(0, WIDE, LANES):
                far = jnp.maximum(
                    far, score_ref[:, pl.ds(at + left, LANES)] + head[:, left : left + LANES]
                )
            far_ref[...] = far
        return carry

    lax.fori_loop(0, quarter // WIDE, score_step, 0)
    head_ref[...] = jnp.broadcast_to(start_ref[...], (8, all_atoms))
    for block in range(blocks):
        span = slice(block * LANES, (block + 1) * LANES)
        far = far_refs[0][span, :]
        for far_ref in far_refs[1:]:
            far = jnp.maximum(far, far_ref[span, :])
        peak = jnp.max(far, axis=1, keepdims=True)
        near_ref[span, :] = jnp.broadcast_to(peak, (LANES, LANES))
        peak_ref[:, span] = rowify(peak, eye)

    def plan_step(step, carry):
        for group in range(2):
            at = pl.multiple_of(step * 32 + group * 16, 16)
            masses = [jnp.zeros((8, LANES), jnp.float32) for _ in range(2)]
            near = [near_ref[pl.ds(at + 8 * side, 8), :] for side in range(2)]
            for left in range(0, all_atoms, LANES):
                part, inner = divmod(left, quarter)
                shares = []
                for side in range(2):
                    score = score_refs[part][pl.ds(at + 8 * side, 8), inner : inner + LANES]
                    share = jnp.exp2(score + head_ref[:, left : left + LANES] - near[side])
                    masses[side] += share
                    shares.append(share)
                plan_ref[pl.ds(at, 16), left : left + LANES] = jnp.concatenate(
                    shares, axis=0
                ).astype(plan_ref.dtype)
            for side in range(2):
                mass_ref[pl.ds(at + 8 * side, 8), :] = masses[side]
        return carry

    lax.fori_loop(0, slots // 32, plan_step, 0)
    copies = sent_ref.shape[0]
    for block in range(blocks):
        span = slice(block * LANES, (block + 1) * LANES)
        mass = jnp.sum(mass_ref[span, :], axis=1, keepdims=True)
        extent = peak_ref[:, span] + jnp.log(rowify(mass, eye)) * LOG2E
        for copy in range(copies):
            sent_ref[copy, :, span] = extent
    own_logits = own_logit_ref[...] * LOG2E
    other_logits = other_logit_ref[...] * LOG2E
    top = jnp.max(jnp.maximum(own_logits, other_logits), axis=1, keepdims=True)
    whole = jnp.sum(jnp.exp2(own_logits - top) + jnp.exp2(other_logits - top), axis=1, keepdims=True)
    whole = top + jnp.log(whole) * LOG2E
    for copy in range(copies):
        sent_ref[copy, :, slots:] = jnp.broadcast_to(whole, (1, LANES))


def pieces(row):
    high = row.astype(jnp.bfloat16).astype(jnp.float32)
    line = lax.broadcasted_iota(jnp.int32, (8, row.shape[1]), 0)
    return jnp.where(line == 0, high, jnp.where(line == 1, row - high, 0.0)).astype(jnp.bfloat16)


def column_sums(weights, plan_ref, left, wide):
    sums = jnp.dot(weights, plan_ref[:, left : left + wide], preferred_element_type=jnp.float32)
    return jnp.sum(sums, axis=0, keepdims=True)


def second_kernel(
    core_ref, count_ref, got_ref, peak_ref, plan_ref, start_ref, own_logit_ref, other_logit_ref,
    sent_ref, scale_ref, base_ref, gain_ref, own_col_ref, other_col_ref,
):
    slots, all_atoms = plan_ref.shape
    atoms = all_atoms // 2
    copies = got_ref.shape[0]
    top = got_ref[0]
    for copy in range(1, copies):
        top = jnp.maximum(top, got_ref[copy])
    mass = jnp.zeros_like(top)
    for copy in range(copies):
        mass += jnp.exp2(got_ref[copy] - top)
    extent = top + jnp.log(mass) * LOG2E
    whole = extent[:, slots : slots + 1]
    extent = extent[:, :slots]
    count = own_count(core_ref, count_ref)
    live = lax.broadcasted_iota(jnp.int32, (1, slots), 1) < count
    words = jnp.full((1, slots), count, jnp.int32).astype(jnp.float32)
    scale = jnp.where(live, jnp.exp2(peak_ref[...] - extent) / words, 0.0)
    scale_ref[...] = scale
    base_ref[...] = (2.0 * EPS * LN2) * whole - EPS * jnp.log(words) - (EPS * LN2) * extent
    weights = pieces(scale)
    part = jnp.zeros((8, slots), jnp.float32)
    wide = min(512, atoms)
    for left in range(0, all_atoms, wide):
        half, inner = divmod(left, atoms)
        logit_ref = (own_logit_ref, other_logit_ref)[half]
        col_ref = (own_col_ref, other_col_ref)[half]
        total = column_sums(weights, plan_ref, left, wide)
        gain_log = logit_ref[:, inner : inner + wide] - jnp.log(total)
        gain_ref[:, left : left + wide] = gain_log
        col_ref[:, inner : inner + wide] = EPS * (
            LN2 * start_ref[:, left : left + wide] + gain_log
        ) - (2.0 * EPS * LN2) * whole
        part += lax.dot_general(
            pieces(jnp.exp(gain_log)), plan_ref[:, left : left + wide], NT,
            preferred_element_type=jnp.float32,
        )
    part = jnp.sum(part, axis=0, keepdims=True) * scale
    for copy in range(copies):
        sent_ref[copy] = part


def third_kernel(
    core_ref, count_ref, got_ref, scale_ref, base_ref, plan_ref, gain_ref, other_col_ref,
    sent_ref, pass_ref,
):
    slots, all_atoms = plan_ref.shape
    atoms = all_atoms // 2
    mass = got_ref[0]
    for copy in range(1, got_ref.shape[0]):
        mass += got_ref[copy]
    core = core_ref[0]
    count = own_count(core_ref, count_ref)
    live = lax.broadcasted_iota(jnp.int32, (1, slots), 1) < count
    words = jnp.full((1, slots), count, jnp.int32).astype(jnp.float32)
    mass = jnp.where(live, mass, 1.0) * words
    pass_ref[:, :slots] = jnp.where(live, base_ref[...] - EPS * jnp.log(mass), 0.0)
    pass_ref[:, slots:] = other_col_ref[...]
    weights = pieces(scale_ref[...] / mass)
    wide = min(512, atoms)
    for left in range(0, all_atoms, wide):
        half, inner = divmod(left, atoms)
        total = column_sums(weights, plan_ref, left, wide)
        marginal = gain_ref[:, left : left + wide] + jnp.log(total)
        place = core if half == 0 else 1 - core
        for group in range(sent_ref.shape[0] // 2):
            sent_ref[2 * group + place, :, inner : inner + wide] = marginal


def mean_kernel(documents, got_ref, mean_ref, sent_ref):
    total = got_ref[0]
    for copy in range(1, got_ref.shape[0]):
        total += got_ref[copy]
    mean = total * (1.0 / documents)
    mean_ref[...] = mean
    top = jnp.max(mean, axis=1, keepdims=True)
    extent = top + jnp.log(jnp.sum(jnp.exp(mean - top), axis=1, keepdims=True))
    for copy in range(sent_ref.shape[0]):
        sent_ref[copy] = jnp.broadcast_to(extent, (1, LANES))


def final_kernel(got_ref, mean_ref, new_ref):
    top = got_ref[0]
    for copy in range(1, got_ref.shape[0]):
        top = jnp.maximum(top, got_ref[copy])
    mass = jnp.zeros_like(top)
    for copy in range(got_ref.shape[0]):
        mass += jnp.exp(got_ref[copy] - top)
    extent = top + jnp.log(mass)
    new_ref[...] = mean_ref[...] - extent[:, :1]


def output_kernel(core_ref, pass_ref, back_ref, own_col_ref, atom_ref, row_ref, col_ref):
    slots = row_ref.shape[1]
    atom = atom_ref[...].astype(jnp.float32)
    square = jnp.sum(atom * atom, axis=0, keepdims=True)
    core = core_ref[0]
    own, other = pass_ref[:, :slots], back_ref[:, :slots]
    own_col, other_col = own_col_ref[...] + square, back_ref[:, slots:] + square
    row_ref[0:1, :] = jnp.where(core == 0, own, other)
    row_ref[1:2, :] = jnp.where(core == 0, other, own)
    col_ref[0:1, :] = jnp.where(core == 0, own_col, other_col)
    col_ref[1:2, :] = jnp.where(core == 0, other_col, own_col)


def swap(x, axis, lists=None):
    return lax.all_to_all(
        x, axis, split_axis=0, concat_axis=0, tiled=True, axis_index_groups=lists
    )


def shards(vocab_table, support_atoms, weight_logits, word_counts, word_shard, word_row):
    groups = lax.axis_size("docs")
    parts = lax.axis_size("supp")
    docs = word_counts.shape[0]
    slots = word_row.shape[0]
    doc_slots = slots // docs
    atoms, width = support_atoms.shape
    core = (lax.axis_index("supp") & 1).astype(jnp.int32).reshape(1)
    pairs = [(i, i ^ 1) for i in range(parts)]
    same_core = [list(range(side, parts, 2)) for side in range(2)]
    same_level = [
        [doc * parts + level + side for doc in range(groups) for side in range(2)]
        for level in range(0, parts, 2)
    ]

    requests, place = call(
        request_kernel,
        (
            jax.ShapeDtypeStruct((groups, HALF), jnp.int32),
            jax.ShapeDtypeStruct((1, doc_slots), jnp.int32),
        ),
        [SMEM, VMEM, VMEM],
        limit=8,
    )(core, word_shard.reshape(1, slots), word_row.reshape(1, slots))
    asked = swap(requests.reshape(groups, 1, HALF), "docs")
    own_atoms = support_atoms.T
    other_atoms = lax.ppermute(own_atoms, "supp", pairs)
    own_logits = weight_logits.reshape(1, atoms)
    other_logits = lax.ppermute(own_logits, "supp", pairs)
    found = vocab_table[asked.reshape(groups * HALF)]
    own = swap(found.reshape(groups, HALF, width), "docs").reshape(groups * HALF, width)
    other = lax.ppermute(own, "supp", pairs)

    quarters = 4
    quarter = 2 * atoms // quarters
    plan, extent, peak, start = call(
        first_kernel,
        (
            jax.ShapeDtypeStruct((doc_slots, 2 * atoms), jnp.bfloat16),
            f32((parts // 2, 1, doc_slots + LANES)),
            f32((1, doc_slots)),
            f32((1, 2 * atoms)),
        ),
        [SMEM, SMEM] + [VMEM] * 7,
        [
            pltpu.VMEM((doc_slots, 2 * groups * HALF), jnp.bfloat16),
            pltpu.VMEM((doc_slots, width), jnp.bfloat16),
            pltpu.VMEM((doc_slots, LANES), jnp.float32),
            [pltpu.VMEM((doc_slots, quarter), jnp.float32)] * quarters,
            [pltpu.VMEM((doc_slots, LANES), jnp.float32)] * quarters,
            pltpu.VMEM((8, 2 * atoms), jnp.float32),
            pltpu.VMEM((doc_slots, LANES), jnp.float32),
            pltpu.VMEM((doc_slots, LANES), jnp.float32),
        ],
        limit=32,
    )(core, word_counts, own, other, place, own_atoms, other_atoms, own_logits, other_logits)
    extents = swap(extent, "supp", same_core)
    mass, scale, base, gain, own_col, other_col = call(
        second_kernel,
        (
            f32((parts // 2, 1, doc_slots)),
            f32((1, doc_slots)),
            f32((1, doc_slots)),
            f32((1, 2 * atoms)),
            f32((1, atoms)),
            f32((1, atoms)),
        ),
        [SMEM, SMEM] + [VMEM] * 6,
        limit=12,
    )(core, word_counts, extents, peak, plan, start, own_logits, other_logits)
    masses = swap(mass, "supp", same_core)
    marginal, passed = call(
        third_kernel,
        (f32((2 * groups, 1, atoms)), f32((1, doc_slots + atoms))),
        [SMEM, SMEM] + [VMEM] * 6,
        limit=12,
    )(core, word_counts, masses, scale, base, plan, gain, other_col)
    marginals = swap(marginal, ("docs", "supp"), same_level)
    back = lax.ppermute(passed, "supp", pairs)
    mean, part = call(
        lambda *refs: mean_kernel(docs * groups, *refs),
        (f32((1, atoms)), f32((parts, 1, LANES))),
        [VMEM],
        limit=8,
    )(marginals)
    shares = swap(part, "supp")
    row_pot, col_pot = call(
        output_kernel,
        (f32((docs, doc_slots)), f32((docs, atoms))),
        [SMEM] + [VMEM] * 4,
        limit=8,
    )(core, passed, back, own_col, own_atoms)
    new_log = call(final_kernel, f32((1, atoms)), [VMEM, VMEM], limit=8)(shares, mean)
    return row_pot, col_pot, new_log.reshape(atoms)


def solution(mesh):
    placed = (P("docs", None), P("supp", None), P("supp"), P("docs"), P("docs", None), P("docs"))
    return jax.shard_map(
        shards,
        mesh=mesh,
        in_specs=placed,
        out_specs=(P("docs", None), P("docs", "supp"), P("supp")),
        check_vma=False,
    )
```

```python
import jax
import jax.numpy as jnp
from jax import lax
from jax.experimental import pallas as pl
from jax.experimental.pallas import tpu as pltpu
from jax.sharding import PartitionSpec as P


EPS = 0.05
LOG2E = 1.4426950408889634
LN2 = 0.6931471805599453
CAP = 128
HALF = CAP // 2
LANES = 128
FAR = 1e30
WIDE = 256
TILES = 3
VMEM = pl.BlockSpec(memory_space=pltpu.VMEM)
SMEM = pl.BlockSpec(memory_space=pltpu.SMEM)
NT = (((1,), (1,)), ((), ()))


def call(kernel, out_shape, in_specs, scratch=(), limit=24):
    return pl.pallas_call(
        kernel,
        out_shape=out_shape,
        in_specs=in_specs,
        out_specs=jax.tree.map(lambda _: VMEM, out_shape),
        scratch_shapes=list(scratch),
        compiler_params=pltpu.CompilerParams(vmem_limit_bytes=limit << 20),
    )


def f32(shape):
    return jax.ShapeDtypeStruct(shape, jnp.float32)


def eye_mask():
    rows = lax.broadcasted_iota(jnp.int32, (LANES, LANES), 0)
    cols = lax.broadcasted_iota(jnp.int32, (LANES, LANES), 1)
    return rows == cols


def rowify(column, eye):
    return jnp.sum(jnp.where(eye, column, 0.0), axis=0, keepdims=True)


def colify(row, eye):
    return jnp.sum(jnp.where(eye, row, 0.0), axis=1, keepdims=True)


def request_kernel(core_ref, shard_ref, row_ref, req_ref, pos_ref):
    groups = req_ref.shape[0]
    slots = shard_ref.shape[1]
    doc_slots = pos_ref.shape[1]
    core = core_ref[0]
    tri = (
        lax.broadcasted_iota(jnp.int32, (LANES, LANES), 0)
        <= lax.broadcasted_iota(jnp.int32, (LANES, LANES), 1)
    ).astype(jnp.bfloat16)
    owner_ids = lax.broadcasted_iota(jnp.int32, (groups, LANES), 0)
    seats = lax.broadcasted_iota(jnp.int32, (HALF, LANES), 0) + core * HALF
    seen = jnp.zeros((groups, 1), jnp.float32)
    req = jnp.zeros((2 * groups, HALF), jnp.float32)
    places = []
    for block in range(slots // LANES):
        span = slice(block * LANES, (block + 1) * LANES)
        shard = shard_ref[:, span]
        row = row_ref[span].reshape(1, LANES)
        member = (owner_ids == shard).astype(jnp.float32)
        counted = seen + jnp.dot(member.astype(jnp.bfloat16), tri, preferred_element_type=jnp.float32)
        seen = counted[:, LANES - 1 :]
        rank = jnp.sum(member * (counted - 1.0), axis=0, keepdims=True).astype(jnp.int32)
        seated = (seats == rank).astype(jnp.float32).astype(jnp.bfloat16)
        high = member * (row >> 7).astype(jnp.float32)
        low = member * (row & 127).astype(jnp.float32)
        both = jnp.concatenate([high, low], axis=0).astype(jnp.bfloat16)
        req += lax.dot_general(both, seated, NT, preferred_element_type=jnp.float32)
        side = (rank >> 6) ^ core
        places.append(side * (groups * HALF) + shard * HALF + (rank & (HALF - 1)))
    req_ref[...] = (req[:groups] * 128.0 + req[groups:]).astype(jnp.int32)
    own_blocks = doc_slots // LANES
    for block in range(own_blocks):
        span = slice(block * LANES, (block + 1) * LANES)
        pos_ref[:, span] = jnp.where(core == 0, places[block], places[own_blocks + block])


def lookup_kernel(asked_ref, vocab_ref, found_ref, table_ref, line_ref):
    width, rows = vocab_ref.shape
    groups = asked_ref.shape[0]
    seats = asked_ref.shape[2]
    count = found_ref.shape[0]
    sides = lax.broadcasted_iota(jnp.int32, (WIDE, WIDE), 0)
    same = (sides == lax.broadcasted_iota(jnp.int32, (WIDE, WIDE), 1)).astype(jnp.float32)
    same = same.astype(jnp.bfloat16)
    tiles = [(tile, min(LANES, width - tile * LANES)) for tile in range(TILES)]

    def spread(first, some):
        turned = lax.dot_general(
            same[:some, :some], vocab_ref[:, pl.ds(first, some)], NT,
            preferred_element_type=jnp.float32,
        )
        for tile, lanes in tiles:
            left = tile * LANES
            table_ref[pl.ds(first * TILES + tile, some, stride=TILES), :lanes] = turned[
                :, left : left + lanes
            ]

    for first in range(0, rows, WIDE):
        spread(first, min(WIDE, rows - first))

    def line_step(group, carry):
        first = pl.multiple_of(group * (seats * TILES), 8)
        for seat in range(seats):
            row = asked_ref[group, 0, seat]
            line_ref[pl.ds(first + seat * TILES, 8), :] = table_ref[pl.ds(row * TILES, 8), :]
        return carry

    lax.fori_loop(0, groups, line_step, 0)
    for tile, lanes in tiles:
        found_ref[:, tile * LANES : (tile + 1) * LANES] = line_ref[
            pl.ds(tile, count, stride=TILES), :
        ].astype(found_ref.dtype)


def own_count(core_ref, count_ref):
    return jnp.where(core_ref[0] == 0, count_ref[0], count_ref[1])


def first_kernel(
    core_ref, count_ref, own_ref, other_ref, pos_ref,
    own_atom_ref, other_atom_ref, own_logit_ref, other_logit_ref,
    plan_ref, sent_ref, peak_ref, start_ref,
    hot_ref, word_ref, square_ref, score_ref, far_ref, head_ref, near_ref, mass_ref,
):
    slots, all_atoms = plan_ref.shape
    half_rows = own_ref.shape[0]
    blocks = slots // LANES
    count = own_count(core_ref, count_ref)
    eye = eye_mask()
    seats = lax.broadcasted_iota(jnp.int32, (LANES, 2 * half_rows), 1).astype(jnp.float32)
    for block in range(blocks):
        span = slice(block * LANES, (block + 1) * LANES)
        place = colify(pos_ref[:, span].astype(jnp.float32), eye)
        hot_ref[span, :] = (seats == place).astype(jnp.float32).astype(jnp.bfloat16)
    words = jnp.dot(hot_ref[:, :half_rows], own_ref[...], preferred_element_type=jnp.float32)
    words += jnp.dot(hot_ref[:, half_rows:], other_ref[...], preferred_element_type=jnp.float32)
    words = words[:, : word_ref.shape[1]]
    square = jnp.sum(words * words, axis=1, keepdims=True) * (LOG2E / EPS)
    slot = lax.broadcasted_iota(jnp.int32, (slots, 1), 0)
    square = jnp.where(slot < count, square, FAR)
    square_ref[...] = jnp.broadcast_to(square, (slots, LANES))
    word_ref[...] = words.astype(jnp.bfloat16)
    far_ref[...] = jnp.full(far_ref.shape, -jnp.inf, jnp.float32)
    atoms = all_atoms // 2
    chunks = all_atoms // WIDE

    def multiply(chunk):
        half, left = divmod(chunk * WIDE, atoms)
        atom_ref = (own_atom_ref, other_atom_ref)[half]
        product = jnp.dot(
            word_ref[...], atom_ref[:, left : left + WIDE], preferred_element_type=jnp.float32
        )
        tops = []
        for inner in range(0, WIDE, LANES):
            at = chunk * WIDE + inner
            score = product[:, inner : inner + LANES] * (2.0 * LOG2E / EPS) - square_ref[...]
            score_ref[:, at : at + LANES] = score
            tops.append(jnp.max(score, axis=0, keepdims=True))
        return tops

    def finish(chunk, tops):
        half, left = divmod(chunk * WIDE, atoms)
        logit_ref = (own_logit_ref, other_logit_ref)[half]
        totals = []
        for tile, top in enumerate(tops):
            at = chunk * WIDE + tile * LANES
            share = jnp.exp2(score_ref[:, at : at + LANES] - top)
            totals.append(jnp.sum(share, axis=0, keepdims=True))
        top = jnp.concatenate(tops, axis=1)
        total = jnp.concatenate(totals, axis=1)
        head = logit_ref[:, left : left + WIDE] * LOG2E - top - jnp.log(total) * LOG2E
        start_ref[:, chunk * WIDE : (chunk + 1) * WIDE] = head

    def reach(chunk, some):
        for group in range(slots // 8):
            lines = slice(group * 8, group * 8 + 8)
            far = far_ref[lines, :]
            for left in range(chunk * WIDE, (chunk + some) * WIDE, LANES):
                far = jnp.maximum(
                    far, score_ref[lines, left : left + LANES] + start_ref[:, left : left + LANES]
                )
            far_ref[lines, :] = far

    waiting = multiply(0)
    for chunk in range(1, chunks):
        coming = multiply(chunk)
        finish(chunk - 1, waiting)
        if chunk % 4 == 1 and chunk > 4:
            reach(chunk - 5, 4)
        waiting = coming
    finish(chunks - 1, waiting)
    reach(chunks - 4, 4)
    head_ref[...] = jnp.broadcast_to(start_ref[...], (8, all_atoms))
    for block in range(blocks):
        span = slice(block * LANES, (block + 1) * LANES)
        peak = jnp.max(far_ref[span, :], axis=1, keepdims=True)
        near_ref[span, :] = jnp.broadcast_to(peak, (LANES, LANES))
        peak_ref[:, span] = rowify(peak, eye)

    def plan_step(step, carry):
        for group in range(4):
            at = pl.multiple_of(step * 64 + group * 16, 16)
            masses = [jnp.zeros((8, LANES), jnp.float32) for _ in range(2)]
            near = [near_ref[pl.ds(at + 8 * side, 8), :] for side in range(2)]
            for left in range(0, all_atoms, LANES):
                shares = []
                for side in range(2):
                    score = score_ref[pl.ds(at + 8 * side, 8), left : left + LANES]
                    share = jnp.exp2(score + head_ref[:, left : left + LANES] - near[side])
                    masses[side] += share
                    shares.append(share)
                plan_ref[pl.ds(at, 16), left : left + LANES] = jnp.concatenate(
                    shares, axis=0
                ).astype(plan_ref.dtype)
            for side in range(2):
                mass_ref[pl.ds(at + 8 * side, 8), :] = masses[side]
        return carry

    lax.fori_loop(0, slots // 64, plan_step, 0)
    copies = sent_ref.shape[0]
    for block in range(blocks):
        span = slice(block * LANES, (block + 1) * LANES)
        mass = jnp.sum(mass_ref[span, :], axis=1, keepdims=True)
        extent = peak_ref[:, span] + jnp.log(rowify(mass, eye)) * LOG2E
        for copy in range(copies):
            sent_ref[copy, :, span] = extent
    own_logits = own_logit_ref[...] * LOG2E
    other_logits = other_logit_ref[...] * LOG2E
    top = jnp.max(jnp.maximum(own_logits, other_logits), axis=1, keepdims=True)
    whole = jnp.sum(jnp.exp2(own_logits - top) + jnp.exp2(other_logits - top), axis=1, keepdims=True)
    whole = top + jnp.log(whole) * LOG2E
    for copy in range(copies):
        sent_ref[copy, :, slots:] = jnp.broadcast_to(whole, (1, LANES))


def pieces(row):
    high = row.astype(jnp.bfloat16).astype(jnp.float32)
    line = lax.broadcasted_iota(jnp.int32, (8, row.shape[1]), 0)
    return jnp.where(line == 0, high, jnp.where(line == 1, row - high, 0.0)).astype(jnp.bfloat16)


def column_sums(weights, plan_ref, left, wide):
    sums = jnp.dot(weights, plan_ref[:, left : left + wide], preferred_element_type=jnp.float32)
    return jnp.sum(sums, axis=0, keepdims=True)


def second_kernel(
    core_ref, count_ref, got_ref, peak_ref, plan_ref, start_ref, own_logit_ref, other_logit_ref,
    sent_ref, scale_ref, base_ref, gain_ref, own_col_ref, other_col_ref,
):
    slots, all_atoms = plan_ref.shape
    atoms = all_atoms // 2
    copies = got_ref.shape[0]
    top = got_ref[0]
    for copy in range(1, copies):
        top = jnp.maximum(top, got_ref[copy])
    mass = jnp.zeros_like(top)
    for copy in range(copies):
        mass += jnp.exp2(got_ref[copy] - top)
    extent = top + jnp.log(mass) * LOG2E
    whole = extent[:, slots : slots + 1]
    extent = extent[:, :slots]
    count = own_count(core_ref, count_ref)
    live = lax.broadcasted_iota(jnp.int32, (1, slots), 1) < count
    words = jnp.full((1, slots), count, jnp.int32).astype(jnp.float32)
    scale = jnp.where(live, jnp.exp2(peak_ref[...] - extent) / words, 0.0)
    scale_ref[...] = scale
    base_ref[...] = (2.0 * EPS * LN2) * whole - EPS * jnp.log(words) - (EPS * LN2) * extent
    weights = pieces(scale)
    wide = min(512, atoms)
    lefts = list(range(0, all_atoms, wide))

    def gain_of(left):
        half, inner = divmod(left, atoms)
        logit_ref = (own_logit_ref, other_logit_ref)[half]
        col_ref = (own_col_ref, other_col_ref)[half]
        total = column_sums(weights, plan_ref, left, wide)
        gain_log = logit_ref[:, inner : inner + wide] - jnp.log(total)
        gain_ref[:, left : left + wide] = gain_log
        col_ref[:, inner : inner + wide] = EPS * (
            LN2 * start_ref[:, left : left + wide] + gain_log
        ) - (2.0 * EPS * LN2) * whole
        return pieces(jnp.exp(gain_log))

    def row_sums(left, gain):
        return lax.dot_general(
            gain, plan_ref[:, left : left + wide], NT, preferred_element_type=jnp.float32
        )

    part = jnp.zeros((8, slots), jnp.float32)
    waiting = gain_of(lefts[0])
    for spot in range(1, len(lefts)):
        coming = gain_of(lefts[spot])
        part += row_sums(lefts[spot - 1], waiting)
        waiting = coming
    part += row_sums(lefts[-1], waiting)
    part = jnp.sum(part, axis=0, keepdims=True) * scale
    for copy in range(copies):
        sent_ref[copy] = part


def third_kernel(
    core_ref, count_ref, got_ref, scale_ref, base_ref, plan_ref, gain_ref, other_col_ref,
    sent_ref, pass_ref,
):
    slots, all_atoms = plan_ref.shape
    atoms = all_atoms // 2
    mass = got_ref[0]
    for copy in range(1, got_ref.shape[0]):
        mass += got_ref[copy]
    core = core_ref[0]
    count = own_count(core_ref, count_ref)
    live = lax.broadcasted_iota(jnp.int32, (1, slots), 1) < count
    words = jnp.full((1, slots), count, jnp.int32).astype(jnp.float32)
    mass = jnp.where(live, mass, 1.0) * words
    pass_ref[:, :slots] = jnp.where(live, base_ref[...] - EPS * jnp.log(mass), 0.0)
    pass_ref[:, slots:] = other_col_ref[...]
    weights = pieces(scale_ref[...] / mass)
    wide = min(512, atoms)
    for left in range(0, all_atoms, wide):
        half, inner = divmod(left, atoms)
        total = column_sums(weights, plan_ref, left, wide)
        marginal = gain_ref[:, left : left + wide] + jnp.log(total)
        place = core if half == 0 else 1 - core
        for group in range(sent_ref.shape[0] // 2):
            sent_ref[2 * group + place, :, inner : inner + wide] = marginal


def mean_kernel(documents, got_ref, mean_ref, sent_ref):
    total = got_ref[0]
    for copy in range(1, got_ref.shape[0]):
        total += got_ref[copy]
    mean = total * (1.0 / documents)
    mean_ref[...] = mean
    top = jnp.max(mean, axis=1, keepdims=True)
    extent = top + jnp.log(jnp.sum(jnp.exp(mean - top), axis=1, keepdims=True))
    for copy in range(sent_ref.shape[0]):
        sent_ref[copy] = jnp.broadcast_to(extent, (1, LANES))


def final_kernel(got_ref, mean_ref, new_ref):
    top = got_ref[0]
    for copy in range(1, got_ref.shape[0]):
        top = jnp.maximum(top, got_ref[copy])
    mass = jnp.zeros_like(top)
    for copy in range(got_ref.shape[0]):
        mass += jnp.exp(got_ref[copy] - top)
    extent = top + jnp.log(mass)
    new_ref[...] = mean_ref[...] - extent[:, :1]


def output_kernel(core_ref, pass_ref, back_ref, own_col_ref, atom_ref, row_ref, col_ref):
    slots = row_ref.shape[1]
    atom = atom_ref[...].astype(jnp.float32)
    square = jnp.sum(atom * atom, axis=0, keepdims=True)
    core = core_ref[0]
    own, other = pass_ref[:, :slots], back_ref[:, :slots]
    own_col, other_col = own_col_ref[...] + square, back_ref[:, slots:] + square
    row_ref[0:1, :] = jnp.where(core == 0, own, other)
    row_ref[1:2, :] = jnp.where(core == 0, other, own)
    col_ref[0:1, :] = jnp.where(core == 0, own_col, other_col)
    col_ref[1:2, :] = jnp.where(core == 0, other_col, own_col)


def swap(x, axis, lists=None):
    return lax.all_to_all(
        x, axis, split_axis=0, concat_axis=0, tiled=True, axis_index_groups=lists
    )


def shards(vocab_table, support_atoms, weight_logits, word_counts, word_shard, word_row):
    groups = lax.axis_size("docs")
    parts = lax.axis_size("supp")
    docs = word_counts.shape[0]
    slots = word_row.shape[0]
    doc_slots = slots // docs
    atoms, width = support_atoms.shape
    core = (lax.axis_index("supp") & 1).astype(jnp.int32).reshape(1)
    pairs = [(i, i ^ 1) for i in range(parts)]
    same_core = [list(range(side, parts, 2)) for side in range(2)]
    same_level = [
        [doc * parts + level + side for doc in range(groups) for side in range(2)]
        for level in range(0, parts, 2)
    ]

    requests, place = call(
        request_kernel,
        (
            jax.ShapeDtypeStruct((groups, HALF), jnp.int32),
            jax.ShapeDtypeStruct((1, doc_slots), jnp.int32),
        ),
        [SMEM, VMEM, VMEM],
        limit=8,
    )(core, word_shard.reshape(1, slots), word_row)
    asked = swap(requests.reshape(groups, 1, HALF), "docs")
    own_atoms = support_atoms.T
    other_atoms = lax.ppermute(own_atoms, "supp", pairs)
    own_logits = weight_logits.reshape(1, atoms)
    other_logits = lax.ppermute(own_logits, "supp", pairs)
    found = call(
        lookup_kernel,
        jax.ShapeDtypeStruct((groups * HALF, TILES * LANES), jnp.bfloat16),
        [SMEM, VMEM],
        [
            pltpu.VMEM(((vocab_table.shape[0] + 8) // 8 * 8 * TILES, LANES), jnp.float32),
            pltpu.VMEM((groups * HALF * TILES + 8, LANES), jnp.float32),
        ],
        limit=24,
    )(asked, vocab_table.T)
    own = swap(found.reshape(groups, HALF, TILES * LANES), "docs")
    own = own.reshape(groups * HALF, TILES * LANES)
    own, other_logits = lax.optimization_barrier((own, other_logits))
    other = lax.ppermute(own, "supp", pairs)

    plan, extent, peak, start = call(
        first_kernel,
        (
            jax.ShapeDtypeStruct((doc_slots, 2 * atoms), jnp.bfloat16),
            f32((parts // 2, 1, doc_slots + LANES)),
            f32((1, doc_slots)),
            f32((1, 2 * atoms)),
        ),
        [SMEM, SMEM] + [VMEM] * 7,
        [
            pltpu.VMEM((doc_slots, 2 * groups * HALF), jnp.bfloat16),
            pltpu.VMEM((doc_slots, width), jnp.bfloat16),
            pltpu.VMEM((doc_slots, LANES), jnp.float32),
            pltpu.VMEM((doc_slots, 2 * atoms), jnp.float32),
            pltpu.VMEM((doc_slots, LANES), jnp.float32),
            pltpu.VMEM((8, 2 * atoms), jnp.float32),
            pltpu.VMEM((doc_slots, LANES), jnp.float32),
            pltpu.VMEM((doc_slots, LANES), jnp.float32),
        ],
        limit=32,
    )(core, word_counts, own, other, place, own_atoms, other_atoms, own_logits, other_logits)
    extents = swap(extent, "supp", same_core)
    mass, scale, base, gain, own_col, other_col = call(
        second_kernel,
        (
            f32((parts // 2, 1, doc_slots)),
            f32((1, doc_slots)),
            f32((1, doc_slots)),
            f32((1, 2 * atoms)),
            f32((1, atoms)),
            f32((1, atoms)),
        ),
        [SMEM, SMEM] + [VMEM] * 6,
        limit=12,
    )(core, word_counts, extents, peak, plan, start, own_logits, other_logits)
    masses = swap(mass, "supp", same_core)
    marginal, passed = call(
        third_kernel,
        (f32((2 * groups, 1, atoms)), f32((1, doc_slots + atoms))),
        [SMEM, SMEM] + [VMEM] * 6,
        limit=12,
    )(core, word_counts, masses, scale, base, plan, gain, other_col)
    marginals = swap(marginal, ("docs", "supp"), same_level)
    back = lax.ppermute(passed, "supp", pairs)
    mean, part = call(
        lambda *refs: mean_kernel(docs * groups, *refs),
        (f32((1, atoms)), f32((parts, 1, LANES))),
        [VMEM],
        limit=8,
    )(marginals)
    shares = swap(part, "supp")
    row_pot, col_pot = call(
        output_kernel,
        (f32((docs, doc_slots)), f32((docs, atoms))),
        [SMEM] + [VMEM] * 4,
        limit=8,
    )(core, passed, back, own_col, own_atoms)
    new_log = call(final_kernel, f32((1, atoms)), [VMEM, VMEM], limit=8)(shares, mean)
    return row_pot, col_pot, new_log.reshape(atoms)


def solution(mesh):
    placed = (P("docs", None), P("supp", None), P("supp"), P("docs"), P("docs", None), P("docs"))
    return jax.shard_map(
        shards,
        mesh=mesh,
        in_specs=placed,
        out_specs=(P("docs", None), P("docs", "supp"), P("supp")),
        check_vma=False,
    )
```

```python
import jax
import jax.numpy as jnp
from jax import lax
from jax.experimental import pallas as pl
from jax.experimental.pallas import tpu as pltpu
from jax.sharding import PartitionSpec as P


EPS = 0.05
LOG2E = 1.4426950408889634
LN2 = 0.6931471805599453
CAP = 128
HALF = CAP // 2
LANES = 128
FAR = 1e30
WIDE = 256
TILES = 3
VMEM = pl.BlockSpec(memory_space=pltpu.VMEM)
SMEM = pl.BlockSpec(memory_space=pltpu.SMEM)
NT = (((1,), (1,)), ((), ()))


def call(kernel, out_shape, in_specs, scratch=(), limit=24):
    return pl.pallas_call(
        kernel,
        out_shape=out_shape,
        in_specs=in_specs,
        out_specs=jax.tree.map(lambda _: VMEM, out_shape),
        scratch_shapes=list(scratch),
        compiler_params=pltpu.CompilerParams(vmem_limit_bytes=limit << 20),
    )


def f32(shape):
    return jax.ShapeDtypeStruct(shape, jnp.float32)


def eye_mask():
    rows = lax.broadcasted_iota(jnp.int32, (LANES, LANES), 0)
    cols = lax.broadcasted_iota(jnp.int32, (LANES, LANES), 1)
    return rows == cols


def rowify(column, eye):
    return jnp.sum(jnp.where(eye, column, 0.0), axis=0, keepdims=True)


def colify(row, eye):
    return jnp.sum(jnp.where(eye, row, 0.0), axis=1, keepdims=True)


def request_kernel(
    core_ref, shard_ref, row_ref, source_ref, req_ref, pos_ref, vocab_ref, sem,
):
    vocab_copy = pltpu.make_async_copy(source_ref, vocab_ref, sem)
    vocab_copy.start()
    groups = req_ref.shape[0]
    slots = shard_ref.shape[1]
    doc_slots = pos_ref.shape[1]
    core = core_ref[0]
    tri = (
        lax.broadcasted_iota(jnp.int32, (LANES, LANES), 0)
        <= lax.broadcasted_iota(jnp.int32, (LANES, LANES), 1)
    ).astype(jnp.bfloat16)
    owner_ids = lax.broadcasted_iota(jnp.int32, (groups, LANES), 0)
    seats = lax.broadcasted_iota(jnp.int32, (HALF, LANES), 0) + core * HALF
    seen = jnp.zeros((groups, 1), jnp.float32)
    req = jnp.zeros((2 * groups, HALF), jnp.float32)
    places = []
    for block in range(slots // LANES):
        span = slice(block * LANES, (block + 1) * LANES)
        shard = shard_ref[:, span]
        row = row_ref[span].reshape(1, LANES)
        member = (owner_ids == shard).astype(jnp.float32)
        counted = seen + jnp.dot(member.astype(jnp.bfloat16), tri, preferred_element_type=jnp.float32)
        seen = counted[:, LANES - 1 :]
        rank = jnp.sum(member * (counted - 1.0), axis=0, keepdims=True).astype(jnp.int32)
        seated = (seats == rank).astype(jnp.float32).astype(jnp.bfloat16)
        high = member * (row >> 7).astype(jnp.float32)
        low = member * (row & 127).astype(jnp.float32)
        both = jnp.concatenate([high, low], axis=0).astype(jnp.bfloat16)
        req += lax.dot_general(both, seated, NT, preferred_element_type=jnp.float32)
        side = (rank >> 6) ^ core
        places.append(side * (groups * HALF) + shard * HALF + (rank & (HALF - 1)))
    req_ref[...] = (req[:groups] * 128.0 + req[groups:]).astype(jnp.int32)
    own_blocks = doc_slots // LANES
    for block in range(own_blocks):
        span = slice(block * LANES, (block + 1) * LANES)
        pos_ref[:, span] = jnp.where(core == 0, places[block], places[own_blocks + block])
    vocab_copy.wait()


def lookup_kernel(asked_ref, vocab_ref, found_ref, table_ref, line_ref):
    width, rows = vocab_ref.shape
    groups = asked_ref.shape[0]
    seats = asked_ref.shape[2]
    count = found_ref.shape[0]
    tiles = [(tile, min(LANES, width - tile * LANES)) for tile in range(TILES)]

    def spread(first, some):
        turned = vocab_ref[:, pl.ds(first, some)].astype(jnp.float32).T
        for tile, lanes in tiles:
            left = tile * LANES
            table_ref[pl.ds(first * TILES + tile, some, stride=TILES), :lanes] = turned[
                :, left : left + lanes
            ]

    for first in range(0, rows, WIDE):
        spread(first, min(WIDE, rows - first))

    def line_step(group, carry):
        first = pl.multiple_of(group * (seats * TILES), 8)
        for seat in range(seats):
            row = asked_ref[group, 0, seat]
            line_ref[pl.ds(first + seat * TILES, 8), :] = table_ref[pl.ds(row * TILES, 8), :]
        return carry

    lax.fori_loop(0, groups, line_step, 0)
    for tile, lanes in tiles:
        found_ref[:, tile * LANES : (tile + 1) * LANES] = line_ref[
            pl.ds(tile, count, stride=TILES), :
        ].astype(found_ref.dtype)


def own_count(core_ref, count_ref):
    return jnp.where(core_ref[0] == 0, count_ref[0], count_ref[1])


def first_kernel(
    core_ref, count_ref, own_ref, other_ref, pos_ref,
    own_atom_ref, other_atom_ref, own_logit_ref, other_logit_ref,
    plan_ref, sent_ref, peak_ref, start_ref,
    hot_ref, word_ref, square_ref, score_ref, far_ref, head_ref, near_ref, mass_ref,
):
    slots, all_atoms = plan_ref.shape
    half_rows = own_ref.shape[0]
    blocks = slots // LANES
    count = own_count(core_ref, count_ref)
    eye = eye_mask()
    seats = lax.broadcasted_iota(jnp.int32, (LANES, 2 * half_rows), 1).astype(jnp.float32)
    for block in range(blocks):
        span = slice(block * LANES, (block + 1) * LANES)
        place = colify(pos_ref[:, span].astype(jnp.float32), eye)
        hot_ref[span, :] = (seats == place).astype(jnp.float32).astype(jnp.bfloat16)
    words = jnp.dot(hot_ref[:, :half_rows], own_ref[...], preferred_element_type=jnp.float32)
    words += jnp.dot(hot_ref[:, half_rows:], other_ref[...], preferred_element_type=jnp.float32)
    words = words[:, : word_ref.shape[1]]
    square = jnp.sum(words * words, axis=1, keepdims=True) * (LOG2E / EPS)
    slot = lax.broadcasted_iota(jnp.int32, (slots, 1), 0)
    square = jnp.where(slot < count, square, FAR)
    square_ref[...] = jnp.broadcast_to(square, (slots, LANES))
    word_ref[...] = words.astype(jnp.bfloat16)
    far_ref[...] = jnp.full(far_ref.shape, -jnp.inf, jnp.float32)
    atoms = all_atoms // 2
    chunks = all_atoms // WIDE

    def multiply(chunk):
        half, left = divmod(chunk * WIDE, atoms)
        atom_ref = (own_atom_ref, other_atom_ref)[half]
        product = jnp.dot(
            word_ref[...], atom_ref[:, left : left + WIDE], preferred_element_type=jnp.float32
        )
        tops = []
        for inner in range(0, WIDE, LANES):
            at = chunk * WIDE + inner
            score = product[:, inner : inner + LANES] * (2.0 * LOG2E / EPS) - square_ref[...]
            score_ref[:, at : at + LANES] = score
            tops.append(jnp.max(score, axis=0, keepdims=True))
        return tops

    def finish(chunk, tops):
        half, left = divmod(chunk * WIDE, atoms)
        logit_ref = (own_logit_ref, other_logit_ref)[half]
        totals = []
        for tile, top in enumerate(tops):
            at = chunk * WIDE + tile * LANES
            share = jnp.exp2(score_ref[:, at : at + LANES] - top)
            totals.append(jnp.sum(share, axis=0, keepdims=True))
        top = jnp.concatenate(tops, axis=1)
        total = jnp.concatenate(totals, axis=1)
        head = logit_ref[:, left : left + WIDE] * LOG2E - top - jnp.log(total) * LOG2E
        start_ref[:, chunk * WIDE : (chunk + 1) * WIDE] = head

    def reach(chunk, some):
        for group in range(slots // 8):
            lines = slice(group * 8, group * 8 + 8)
            far = far_ref[lines, :]
            for left in range(chunk * WIDE, (chunk + some) * WIDE, LANES):
                far = jnp.maximum(
                    far, score_ref[lines, left : left + LANES] + start_ref[:, left : left + LANES]
                )
            far_ref[lines, :] = far

    waiting = multiply(0)
    for chunk in range(1, chunks):
        coming = multiply(chunk)
        finish(chunk - 1, waiting)
        if chunk % 4 == 1 and chunk > 4:
            reach(chunk - 5, 4)
        waiting = coming
    finish(chunks - 1, waiting)
    reach(chunks - 4, 4)
    head_ref[...] = jnp.broadcast_to(start_ref[...], (8, all_atoms))
    for block in range(blocks):
        span = slice(block * LANES, (block + 1) * LANES)
        peak = jnp.max(far_ref[span, :], axis=1, keepdims=True)
        near_ref[span, :] = jnp.broadcast_to(peak, (LANES, LANES))
        peak_ref[:, span] = rowify(peak, eye)

    def plan_step(step, carry):
        for group in range(4):
            at = pl.multiple_of(step * 64 + group * 16, 16)
            masses = [jnp.zeros((8, LANES), jnp.float32) for _ in range(2)]
            near = [near_ref[pl.ds(at + 8 * side, 8), :] for side in range(2)]
            for left in range(0, all_atoms, LANES):
                shares = []
                for side in range(2):
                    score = score_ref[pl.ds(at + 8 * side, 8), left : left + LANES]
                    share = jnp.exp2(score + head_ref[:, left : left + LANES] - near[side])
                    masses[side] += share
                    shares.append(share)
                plan_ref[pl.ds(at, 16), left : left + LANES] = jnp.concatenate(
                    shares, axis=0
                ).astype(plan_ref.dtype)
            for side in range(2):
                mass_ref[pl.ds(at + 8 * side, 8), :] = masses[side]
        return carry

    lax.fori_loop(0, slots // 64, plan_step, 0)
    copies = sent_ref.shape[0]
    for block in range(blocks):
        span = slice(block * LANES, (block + 1) * LANES)
        mass = jnp.sum(mass_ref[span, :], axis=1, keepdims=True)
        extent = peak_ref[:, span] + jnp.log(rowify(mass, eye)) * LOG2E
        for copy in range(copies):
            sent_ref[copy, :, span] = extent
    own_logits = own_logit_ref[...] * LOG2E
    other_logits = other_logit_ref[...] * LOG2E
    top = jnp.max(jnp.maximum(own_logits, other_logits), axis=1, keepdims=True)
    whole = jnp.sum(jnp.exp2(own_logits - top) + jnp.exp2(other_logits - top), axis=1, keepdims=True)
    whole = top + jnp.log(whole) * LOG2E
    for copy in range(copies):
        sent_ref[copy, :, slots:] = jnp.broadcast_to(whole, (1, LANES))


def pieces(row):
    high = row.astype(jnp.bfloat16).astype(jnp.float32)
    line = lax.broadcasted_iota(jnp.int32, (8, row.shape[1]), 0)
    return jnp.where(line == 0, high, jnp.where(line == 1, row - high, 0.0)).astype(jnp.bfloat16)


def column_sums(weights, plan_ref, left, wide):
    sums = jnp.dot(weights, plan_ref[:, left : left + wide], preferred_element_type=jnp.float32)
    return jnp.sum(sums, axis=0, keepdims=True)


def second_kernel(
    core_ref, count_ref, got_ref, peak_ref, plan_ref, start_ref, own_logit_ref, other_logit_ref,
    sent_ref, scale_ref, base_ref, gain_ref, own_col_ref, other_col_ref,
):
    slots, all_atoms = plan_ref.shape
    atoms = all_atoms // 2
    copies = got_ref.shape[0]
    top = got_ref[0]
    for copy in range(1, copies):
        top = jnp.maximum(top, got_ref[copy])
    mass = jnp.zeros_like(top)
    for copy in range(copies):
        mass += jnp.exp2(got_ref[copy] - top)
    extent = top + jnp.log(mass) * LOG2E
    whole = extent[:, slots : slots + 1]
    extent = extent[:, :slots]
    count = own_count(core_ref, count_ref)
    live = lax.broadcasted_iota(jnp.int32, (1, slots), 1) < count
    words = jnp.full((1, slots), count, jnp.int32).astype(jnp.float32)
    scale = jnp.where(live, jnp.exp2(peak_ref[...] - extent) / words, 0.0)
    scale_ref[...] = scale
    base_ref[...] = (2.0 * EPS * LN2) * whole - EPS * jnp.log(words) - (EPS * LN2) * extent
    weights = pieces(scale)
    wide = min(512, atoms)
    lefts = list(range(0, all_atoms, wide))

    def gain_of(left):
        half, inner = divmod(left, atoms)
        logit_ref = (own_logit_ref, other_logit_ref)[half]
        col_ref = (own_col_ref, other_col_ref)[half]
        total = column_sums(weights, plan_ref, left, wide)
        gain_log = logit_ref[:, inner : inner + wide] - jnp.log(total)
        gain_ref[:, left : left + wide] = gain_log
        col_ref[:, inner : inner + wide] = EPS * (
            LN2 * start_ref[:, left : left + wide] + gain_log
        ) - (2.0 * EPS * LN2) * whole
        return pieces(jnp.exp(gain_log))

    def row_sums(left, gain):
        return lax.dot_general(
            gain, plan_ref[:, left : left + wide], NT, preferred_element_type=jnp.float32
        )

    part = jnp.zeros((8, slots), jnp.float32)
    waiting = gain_of(lefts[0])
    for spot in range(1, len(lefts)):
        coming = gain_of(lefts[spot])
        part += row_sums(lefts[spot - 1], waiting)
        waiting = coming
    part += row_sums(lefts[-1], waiting)
    part = jnp.sum(part, axis=0, keepdims=True) * scale
    for copy in range(copies):
        sent_ref[copy] = part


def third_kernel(
    core_ref, count_ref, got_ref, scale_ref, base_ref, plan_ref, gain_ref, other_col_ref,
    sent_ref, pass_ref,
):
    slots, all_atoms = plan_ref.shape
    atoms = all_atoms // 2
    mass = got_ref[0]
    for copy in range(1, got_ref.shape[0]):
        mass += got_ref[copy]
    core = core_ref[0]
    count = own_count(core_ref, count_ref)
    live = lax.broadcasted_iota(jnp.int32, (1, slots), 1) < count
    words = jnp.full((1, slots), count, jnp.int32).astype(jnp.float32)
    mass = jnp.where(live, mass, 1.0) * words
    pass_ref[:, :slots] = jnp.where(live, base_ref[...] - EPS * jnp.log(mass), 0.0)
    pass_ref[:, slots:] = other_col_ref[...]
    weights = pieces(scale_ref[...] / mass)
    wide = min(512, atoms)
    for left in range(0, all_atoms, wide):
        half, inner = divmod(left, atoms)
        total = column_sums(weights, plan_ref, left, wide)
        marginal = gain_ref[:, left : left + wide] + jnp.log(total)
        place = core if half == 0 else 1 - core
        for group in range(sent_ref.shape[0] // 2):
            sent_ref[2 * group + place, :, inner : inner + wide] = marginal


def mean_kernel(documents, got_ref, mean_ref, sent_ref):
    total = got_ref[0]
    for copy in range(1, got_ref.shape[0]):
        total += got_ref[copy]
    mean = total * (1.0 / documents)
    mean_ref[...] = mean
    top = jnp.max(mean, axis=1, keepdims=True)
    extent = top + jnp.log(jnp.sum(jnp.exp(mean - top), axis=1, keepdims=True))
    for copy in range(sent_ref.shape[0]):
        sent_ref[copy] = jnp.broadcast_to(extent, (1, LANES))


def final_kernel(got_ref, mean_ref, new_ref):
    top = got_ref[0]
    for copy in range(1, got_ref.shape[0]):
        top = jnp.maximum(top, got_ref[copy])
    mass = jnp.zeros_like(top)
    for copy in range(got_ref.shape[0]):
        mass += jnp.exp(got_ref[copy] - top)
    extent = top + jnp.log(mass)
    new_ref[...] = mean_ref[...] - extent[:, :1]


def output_kernel(core_ref, pass_ref, back_ref, own_col_ref, atom_ref, row_ref, col_ref):
    slots = row_ref.shape[1]
    atom = atom_ref[...].astype(jnp.float32)
    square = jnp.sum(atom * atom, axis=0, keepdims=True)
    core = core_ref[0]
    own, other = pass_ref[:, :slots], back_ref[:, :slots]
    own_col, other_col = own_col_ref[...] + square, back_ref[:, slots:] + square
    row_ref[0:1, :] = jnp.where(core == 0, own, other)
    row_ref[1:2, :] = jnp.where(core == 0, other, own)
    col_ref[0:1, :] = jnp.where(core == 0, own_col, other_col)
    col_ref[1:2, :] = jnp.where(core == 0, other_col, own_col)


def swap(x, axis, lists=None):
    return lax.all_to_all(
        x, axis, split_axis=0, concat_axis=0, tiled=True, axis_index_groups=lists
    )


def shards(vocab_table, support_atoms, weight_logits, word_counts, word_shard, word_row):
    groups = lax.axis_size("docs")
    parts = lax.axis_size("supp")
    docs = word_counts.shape[0]
    slots = word_row.shape[0]
    doc_slots = slots // docs
    atoms, width = support_atoms.shape
    core = (lax.axis_index("supp") & 1).astype(jnp.int32).reshape(1)
    pairs = [(i, i ^ 1) for i in range(parts)]
    same_core = [list(range(side, parts, 2)) for side in range(2)]
    same_level = [
        [doc * parts + level + side for doc in range(groups) for side in range(2)]
        for level in range(0, parts, 2)
    ]

    requests, place, vocab = call(
        request_kernel,
        (
            jax.ShapeDtypeStruct((groups, HALF), jnp.int32),
            jax.ShapeDtypeStruct((1, doc_slots), jnp.int32),
            jax.ShapeDtypeStruct(vocab_table.shape[::-1], vocab_table.dtype),
        ),
        [SMEM, VMEM, VMEM, pl.BlockSpec(memory_space=pltpu.HBM)],
        [pltpu.SemaphoreType.DMA],
        limit=48,
    )(core, word_shard.reshape(1, slots), word_row, vocab_table.T)
    asked = swap(requests.reshape(groups, 1, HALF), "docs")
    own_atoms = support_atoms.T
    other_atoms = lax.ppermute(own_atoms, "supp", pairs)
    own_logits = weight_logits.reshape(1, atoms)
    other_logits = lax.ppermute(own_logits, "supp", pairs)
    found = call(
        lookup_kernel,
        jax.ShapeDtypeStruct((groups * HALF, TILES * LANES), jnp.bfloat16),
        [SMEM, VMEM],
        [
            pltpu.VMEM(((vocab_table.shape[0] + 8) // 8 * 8 * TILES, LANES), jnp.float32),
            pltpu.VMEM((groups * HALF * TILES + 8, LANES), jnp.float32),
        ],
        limit=24,
    )(asked, vocab)
    own = swap(found.reshape(groups, HALF, TILES * LANES), "docs")
    own = own.reshape(groups * HALF, TILES * LANES)
    own, other_logits = lax.optimization_barrier((own, other_logits))
    other = lax.ppermute(own, "supp", pairs)

    plan, extent, peak, start = call(
        first_kernel,
        (
            jax.ShapeDtypeStruct((doc_slots, 2 * atoms), jnp.bfloat16),
            f32((parts // 2, 1, doc_slots + LANES)),
            f32((1, doc_slots)),
            f32((1, 2 * atoms)),
        ),
        [SMEM, SMEM] + [VMEM] * 7,
        [
            pltpu.VMEM((doc_slots, 2 * groups * HALF), jnp.bfloat16),
            pltpu.VMEM((doc_slots, width), jnp.bfloat16),
            pltpu.VMEM((doc_slots, LANES), jnp.float32),
            pltpu.VMEM((doc_slots, 2 * atoms), jnp.float32),
            pltpu.VMEM((doc_slots, LANES), jnp.float32),
            pltpu.VMEM((8, 2 * atoms), jnp.float32),
            pltpu.VMEM((doc_slots, LANES), jnp.float32),
            pltpu.VMEM((doc_slots, LANES), jnp.float32),
        ],
        limit=32,
    )(core, word_counts, own, other, place, own_atoms, other_atoms, own_logits, other_logits)
    extents = swap(extent, "supp", same_core)
    mass, scale, base, gain, own_col, other_col = call(
        second_kernel,
        (
            f32((parts // 2, 1, doc_slots)),
            f32((1, doc_slots)),
            f32((1, doc_slots)),
            f32((1, 2 * atoms)),
            f32((1, atoms)),
            f32((1, atoms)),
        ),
        [SMEM, SMEM] + [VMEM] * 6,
        limit=12,
    )(core, word_counts, extents, peak, plan, start, own_logits, other_logits)
    masses = swap(mass, "supp", same_core)
    marginal, passed = call(
        third_kernel,
        (f32((2 * groups, 1, atoms)), f32((1, doc_slots + atoms))),
        [SMEM, SMEM] + [VMEM] * 6,
        limit=12,
    )(core, word_counts, masses, scale, base, plan, gain, other_col)
    marginals = swap(marginal, ("docs", "supp"), same_level)
    back = lax.ppermute(passed, "supp", pairs)
    mean, part = call(
        lambda *refs: mean_kernel(docs * groups, *refs),
        (f32((1, atoms)), f32((parts, 1, LANES))),
        [VMEM],
        limit=8,
    )(marginals)
    shares = swap(part, "supp")
    row_pot, col_pot = call(
        output_kernel,
        (f32((docs, doc_slots)), f32((docs, atoms))),
        [SMEM] + [VMEM] * 4,
        limit=8,
    )(core, passed, back, own_col, own_atoms)
    new_log = call(final_kernel, f32((1, atoms)), [VMEM, VMEM], limit=8)(shares, mean)
    return row_pot, col_pot, new_log.reshape(atoms)


def solution(mesh):
    placed = (P("docs", None), P("supp", None), P("supp"), P("docs"), P("docs", None), P("docs"))
    return jax.shard_map(
        shards,
        mesh=mesh,
        in_specs=placed,
        out_specs=(P("docs", None), P("docs", "supp"), P("supp")),
        check_vma=False,
    )
```

```python
import jax
import jax.numpy as jnp
from jax import lax
from jax.experimental import pallas as pl
from jax.experimental.pallas import tpu as pltpu
from jax.sharding import PartitionSpec as P


EPS = 0.05
LOG2E = 1.4426950408889634
LN2 = 0.6931471805599453
CAP = 128
HALF = CAP // 2
LANES = 128
FAR = 1e30
WIDE = 256
CHUNK = 512
TILES = 3
VMEM = pl.BlockSpec(memory_space=pltpu.VMEM)
SMEM = pl.BlockSpec(memory_space=pltpu.SMEM)
NT = (((1,), (1,)), ((), ()))


def call(kernel, out_shape, in_specs, scratch=(), limit=24):
    return pl.pallas_call(
        kernel,
        out_shape=out_shape,
        in_specs=in_specs,
        out_specs=jax.tree.map(lambda _: VMEM, out_shape),
        scratch_shapes=list(scratch),
        compiler_params=pltpu.CompilerParams(vmem_limit_bytes=limit << 20),
    )


def f32(shape):
    return jax.ShapeDtypeStruct(shape, jnp.float32)


def eye_mask():
    rows = lax.broadcasted_iota(jnp.int32, (LANES, LANES), 0)
    cols = lax.broadcasted_iota(jnp.int32, (LANES, LANES), 1)
    return rows == cols


def rowify(column, eye):
    return jnp.sum(jnp.where(eye, column, 0.0), axis=0, keepdims=True)


def colify(row, eye):
    return jnp.sum(jnp.where(eye, row, 0.0), axis=1, keepdims=True)


def request_kernel(
    core_ref, shard_ref, row_ref, source_ref, req_ref, pos_ref, vocab_ref, sem,
):
    vocab_copy = pltpu.make_async_copy(source_ref, vocab_ref, sem)
    vocab_copy.start()
    groups = req_ref.shape[0]
    slots = shard_ref.shape[1]
    doc_slots = pos_ref.shape[1]
    core = core_ref[0]
    tri = (
        lax.broadcasted_iota(jnp.int32, (LANES, LANES), 0)
        <= lax.broadcasted_iota(jnp.int32, (LANES, LANES), 1)
    ).astype(jnp.bfloat16)
    owner_ids = lax.broadcasted_iota(jnp.int32, (groups, LANES), 0)
    seats = lax.broadcasted_iota(jnp.int32, (HALF, LANES), 0) + core * HALF
    seen = jnp.zeros((groups, 1), jnp.float32)
    req = jnp.zeros((2 * groups, HALF), jnp.float32)
    places = []
    for block in range(slots // LANES):
        span = slice(block * LANES, (block + 1) * LANES)
        shard = shard_ref[:, span]
        row = row_ref[span].reshape(1, LANES)
        member = (owner_ids == shard).astype(jnp.float32)
        counted = seen + jnp.dot(member.astype(jnp.bfloat16), tri, preferred_element_type=jnp.float32)
        seen = counted[:, LANES - 1 :]
        rank = jnp.sum(member * (counted - 1.0), axis=0, keepdims=True).astype(jnp.int32)
        seated = (seats == rank).astype(jnp.float32).astype(jnp.bfloat16)
        high = member * (row >> 7).astype(jnp.float32)
        low = member * (row & 127).astype(jnp.float32)
        both = jnp.concatenate([high, low], axis=0).astype(jnp.bfloat16)
        req += lax.dot_general(both, seated, NT, preferred_element_type=jnp.float32)
        side = (rank >> 6) ^ core
        places.append(side * (groups * HALF) + shard * HALF + (rank & (HALF - 1)))
    req_ref[...] = (req[:groups] * 128.0 + req[groups:]).astype(jnp.int32)
    own_blocks = doc_slots // LANES
    for block in range(own_blocks):
        span = slice(block * LANES, (block + 1) * LANES)
        pos_ref[:, span] = jnp.where(core == 0, places[block], places[own_blocks + block])
    vocab_copy.wait()


def lookup_kernel(asked_ref, vocab_ref, found_ref, table_ref, line_ref):
    width, rows = vocab_ref.shape
    groups = asked_ref.shape[0]
    seats = asked_ref.shape[2]
    count = found_ref.shape[0]
    tiles = [(tile, min(LANES, width - tile * LANES)) for tile in range(TILES)]

    def spread(first, some):
        turned = vocab_ref[:, pl.ds(first, some)].astype(jnp.float32).T
        for tile, lanes in tiles:
            left = tile * LANES
            table_ref[pl.ds(first * TILES + tile, some, stride=TILES), :lanes] = turned[
                :, left : left + lanes
            ]

    for first in range(0, rows, WIDE):
        spread(first, min(WIDE, rows - first))

    def line_step(group, carry):
        first = pl.multiple_of(group * (seats * TILES), 8)
        for seat in range(seats):
            row = asked_ref[group, 0, seat]
            line_ref[pl.ds(first + seat * TILES, 8), :] = table_ref[pl.ds(row * TILES, 8), :]
        return carry

    lax.fori_loop(0, groups, line_step, 0)
    for tile, lanes in tiles:
        found_ref[:, tile * LANES : (tile + 1) * LANES] = line_ref[
            pl.ds(tile, count, stride=TILES), :
        ].astype(found_ref.dtype)


def own_count(core_ref, count_ref):
    return jnp.where(core_ref[0] == 0, count_ref[0], count_ref[1])


def first_kernel(
    core_ref, count_ref, own_ref, other_ref, pos_ref,
    own_atom_ref, other_atom_ref, own_logit_ref, other_logit_ref,
    plan_ref, sent_ref, peak_ref, start_ref,
    hot_ref, word_ref, square_ref, score_ref, far_ref, head_ref, near_ref, mass_ref,
):
    slots, all_atoms = plan_ref.shape
    half_rows = own_ref.shape[0]
    blocks = slots // LANES
    count = own_count(core_ref, count_ref)
    eye = eye_mask()
    seats = lax.broadcasted_iota(jnp.int32, (LANES, 2 * half_rows), 1).astype(jnp.float32)
    for block in range(blocks):
        span = slice(block * LANES, (block + 1) * LANES)
        place = colify(pos_ref[:, span].astype(jnp.float32), eye)
        hot_ref[span, :] = (seats == place).astype(jnp.float32).astype(jnp.bfloat16)
    words = jnp.dot(hot_ref[:, :half_rows], own_ref[...], preferred_element_type=jnp.float32)
    words += jnp.dot(hot_ref[:, half_rows:], other_ref[...], preferred_element_type=jnp.float32)
    words = words[:, : word_ref.shape[1]]
    square = jnp.sum(words * words, axis=1, keepdims=True) * (LOG2E / EPS)
    slot = lax.broadcasted_iota(jnp.int32, (slots, 1), 0)
    square = jnp.where(slot < count, square, FAR)
    square_ref[...] = jnp.broadcast_to(square, (slots, LANES))
    word_ref[...] = words.astype(jnp.bfloat16)
    far_ref[...] = jnp.full(far_ref.shape, -jnp.inf, jnp.float32)
    atoms = all_atoms // 2
    chunks = all_atoms // CHUNK

    def multiply(chunk):
        half, left = divmod(chunk * CHUNK, atoms)
        atom_ref = (own_atom_ref, other_atom_ref)[half]
        product = jnp.dot(
            word_ref[...], atom_ref[:, left : left + CHUNK], preferred_element_type=jnp.float32
        )
        tops = []
        for inner in range(0, CHUNK, LANES):
            at = chunk * CHUNK + inner
            score = product[:, inner : inner + LANES] * (2.0 * LOG2E / EPS) - square_ref[...]
            score_ref[:, at : at + LANES] = score
            tops.append(jnp.max(score, axis=0, keepdims=True))
        return tops

    def finish(chunk, tops):
        half, left = divmod(chunk * CHUNK, atoms)
        logit_ref = (own_logit_ref, other_logit_ref)[half]
        totals = []
        for tile, top in enumerate(tops):
            at = chunk * CHUNK + tile * LANES
            share = jnp.exp2(score_ref[:, at : at + LANES] - top)
            totals.append(jnp.sum(share, axis=0, keepdims=True))
        top = jnp.concatenate(tops, axis=1)
        total = jnp.concatenate(totals, axis=1)
        head = logit_ref[:, left : left + CHUNK] * LOG2E - top - jnp.log(total) * LOG2E
        start_ref[:, chunk * CHUNK : (chunk + 1) * CHUNK] = head

    def reach(chunk, some):
        for group in range(slots // 8):
            lines = slice(group * 8, group * 8 + 8)
            far = far_ref[lines, :]
            for left in range(chunk * CHUNK, (chunk + some) * CHUNK, LANES):
                far = jnp.maximum(
                    far, score_ref[lines, left : left + LANES] + start_ref[:, left : left + LANES]
                )
            far_ref[lines, :] = far

    waiting = multiply(0)
    for chunk in range(1, chunks):
        coming = multiply(chunk)
        finish(chunk - 1, waiting)
        if chunk % 2 == 1 and chunk > 2:
            reach(chunk - 3, 2)
        waiting = coming
    finish(chunks - 1, waiting)
    reach(chunks - 2, 2)
    head_ref[...] = jnp.broadcast_to(start_ref[...], (8, all_atoms))
    for block in range(blocks):
        span = slice(block * LANES, (block + 1) * LANES)
        peak = jnp.max(far_ref[span, :], axis=1, keepdims=True)
        near_ref[span, :] = jnp.broadcast_to(peak, (LANES, LANES))
        peak_ref[:, span] = rowify(peak, eye)

    def plan_step(step, carry):
        for group in range(4):
            at = pl.multiple_of(step * 64 + group * 16, 16)
            masses = [jnp.zeros((8, LANES), jnp.float32) for _ in range(2)]
            near = [near_ref[pl.ds(at + 8 * side, 8), :] for side in range(2)]
            for left in range(0, all_atoms, LANES):
                shares = []
                for side in range(2):
                    score = score_ref[pl.ds(at + 8 * side, 8), left : left + LANES]
                    share = jnp.exp2(score + head_ref[:, left : left + LANES] - near[side])
                    masses[side] += share
                    shares.append(share)
                plan_ref[pl.ds(at, 16), left : left + LANES] = jnp.concatenate(
                    shares, axis=0
                ).astype(plan_ref.dtype)
            for side in range(2):
                mass_ref[pl.ds(at + 8 * side, 8), :] = masses[side]
        return carry

    lax.fori_loop(0, slots // 64, plan_step, 0)
    copies = sent_ref.shape[0]
    for block in range(blocks):
        span = slice(block * LANES, (block + 1) * LANES)
        mass = jnp.sum(mass_ref[span, :], axis=1, keepdims=True)
        extent = peak_ref[:, span] + jnp.log(rowify(mass, eye)) * LOG2E
        for copy in range(copies):
            sent_ref[copy, :, span] = extent
    own_logits = own_logit_ref[...] * LOG2E
    other_logits = other_logit_ref[...] * LOG2E
    top = jnp.max(jnp.maximum(own_logits, other_logits), axis=1, keepdims=True)
    whole = jnp.sum(jnp.exp2(own_logits - top) + jnp.exp2(other_logits - top), axis=1, keepdims=True)
    whole = top + jnp.log(whole) * LOG2E
    for copy in range(copies):
        sent_ref[copy, :, slots:] = jnp.broadcast_to(whole, (1, LANES))


def pieces(row):
    high = row.astype(jnp.bfloat16).astype(jnp.float32)
    line = lax.broadcasted_iota(jnp.int32, (8, row.shape[1]), 0)
    return jnp.where(line == 0, high, jnp.where(line == 1, row - high, 0.0)).astype(jnp.bfloat16)


def column_sums(weights, plan_ref, left, wide):
    sums = jnp.dot(weights, plan_ref[:, left : left + wide], preferred_element_type=jnp.float32)
    return jnp.sum(sums, axis=0, keepdims=True)


def second_kernel(
    core_ref, count_ref, got_ref, peak_ref, plan_ref, start_ref, own_logit_ref, other_logit_ref,
    sent_ref, scale_ref, base_ref, gain_ref, own_col_ref, other_col_ref,
):
    slots, all_atoms = plan_ref.shape
    atoms = all_atoms // 2
    copies = got_ref.shape[0]
    top = got_ref[0]
    for copy in range(1, copies):
        top = jnp.maximum(top, got_ref[copy])
    mass = jnp.zeros_like(top)
    for copy in range(copies):
        mass += jnp.exp2(got_ref[copy] - top)
    extent = top + jnp.log(mass) * LOG2E
    whole = extent[:, slots : slots + 1]
    extent = extent[:, :slots]
    count = own_count(core_ref, count_ref)
    live = lax.broadcasted_iota(jnp.int32, (1, slots), 1) < count
    words = jnp.full((1, slots), count, jnp.int32).astype(jnp.float32)
    scale = jnp.where(live, jnp.exp2(peak_ref[...] - extent) / words, 0.0)
    scale_ref[...] = scale
    base_ref[...] = (2.0 * EPS * LN2) * whole - EPS * jnp.log(words) - (EPS * LN2) * extent
    weights = pieces(scale)
    wide = min(512, atoms)
    lefts = list(range(0, all_atoms, wide))

    def gain_of(left):
        half, inner = divmod(left, atoms)
        logit_ref = (own_logit_ref, other_logit_ref)[half]
        col_ref = (own_col_ref, other_col_ref)[half]
        total = column_sums(weights, plan_ref, left, wide)
        gain_log = logit_ref[:, inner : inner + wide] - jnp.log(total)
        gain_ref[:, left : left + wide] = gain_log
        col_ref[:, inner : inner + wide] = EPS * (
            LN2 * start_ref[:, left : left + wide] + gain_log
        ) - (2.0 * EPS * LN2) * whole
        return pieces(jnp.exp(gain_log))

    def row_sums(left, gain):
        return lax.dot_general(
            gain, plan_ref[:, left : left + wide], NT, preferred_element_type=jnp.float32
        )

    part = jnp.zeros((8, slots), jnp.float32)
    waiting = gain_of(lefts[0])
    for spot in range(1, len(lefts)):
        coming = gain_of(lefts[spot])
        part += row_sums(lefts[spot - 1], waiting)
        waiting = coming
    part += row_sums(lefts[-1], waiting)
    part = jnp.sum(part, axis=0, keepdims=True) * scale
    for copy in range(copies):
        sent_ref[copy] = part


def third_kernel(
    core_ref, count_ref, got_ref, scale_ref, base_ref, plan_ref, gain_ref, other_col_ref,
    sent_ref, pass_ref,
):
    slots, all_atoms = plan_ref.shape
    atoms = all_atoms // 2
    mass = got_ref[0]
    for copy in range(1, got_ref.shape[0]):
        mass += got_ref[copy]
    core = core_ref[0]
    count = own_count(core_ref, count_ref)
    live = lax.broadcasted_iota(jnp.int32, (1, slots), 1) < count
    words = jnp.full((1, slots), count, jnp.int32).astype(jnp.float32)
    mass = jnp.where(live, mass, 1.0) * words
    pass_ref[:, :slots] = jnp.where(live, base_ref[...] - EPS * jnp.log(mass), 0.0)
    pass_ref[:, slots:] = other_col_ref[...]
    weights = pieces(scale_ref[...] / mass)
    wide = min(512, atoms)
    for left in range(0, all_atoms, wide):
        half, inner = divmod(left, atoms)
        total = column_sums(weights, plan_ref, left, wide)
        marginal = gain_ref[:, left : left + wide] + jnp.log(total)
        place = core if half == 0 else 1 - core
        for group in range(sent_ref.shape[0] // 2):
            sent_ref[2 * group + place, :, inner : inner + wide] = marginal


def mean_kernel(documents, got_ref, mean_ref, sent_ref):
    total = got_ref[0]
    for copy in range(1, got_ref.shape[0]):
        total += got_ref[copy]
    mean = total * (1.0 / documents)
    mean_ref[...] = mean
    top = jnp.max(mean, axis=1, keepdims=True)
    extent = top + jnp.log(jnp.sum(jnp.exp(mean - top), axis=1, keepdims=True))
    for copy in range(sent_ref.shape[0]):
        sent_ref[copy] = jnp.broadcast_to(extent, (1, LANES))


def final_kernel(got_ref, mean_ref, new_ref):
    top = got_ref[0]
    for copy in range(1, got_ref.shape[0]):
        top = jnp.maximum(top, got_ref[copy])
    mass = jnp.zeros_like(top)
    for copy in range(got_ref.shape[0]):
        mass += jnp.exp(got_ref[copy] - top)
    extent = top + jnp.log(mass)
    new_ref[...] = mean_ref[...] - extent[:, :1]


def output_kernel(core_ref, pass_ref, back_ref, own_col_ref, atom_ref, row_ref, col_ref):
    slots = row_ref.shape[1]
    atom = atom_ref[...].astype(jnp.float32)
    square = jnp.sum(atom * atom, axis=0, keepdims=True)
    core = core_ref[0]
    own, other = pass_ref[:, :slots], back_ref[:, :slots]
    own_col, other_col = own_col_ref[...] + square, back_ref[:, slots:] + square
    row_ref[0:1, :] = jnp.where(core == 0, own, other)
    row_ref[1:2, :] = jnp.where(core == 0, other, own)
    col_ref[0:1, :] = jnp.where(core == 0, own_col, other_col)
    col_ref[1:2, :] = jnp.where(core == 0, other_col, own_col)


def swap(x, axis, lists=None):
    return lax.all_to_all(
        x, axis, split_axis=0, concat_axis=0, tiled=True, axis_index_groups=lists
    )


def shards(vocab_table, support_atoms, weight_logits, word_counts, word_shard, word_row):
    groups = lax.axis_size("docs")
    parts = lax.axis_size("supp")
    docs = word_counts.shape[0]
    slots = word_row.shape[0]
    doc_slots = slots // docs
    atoms, width = support_atoms.shape
    core = (lax.axis_index("supp") & 1).astype(jnp.int32).reshape(1)
    pairs = [(i, i ^ 1) for i in range(parts)]
    same_core = [list(range(side, parts, 2)) for side in range(2)]
    same_level = [
        [doc * parts + level + side for doc in range(groups) for side in range(2)]
        for level in range(0, parts, 2)
    ]

    requests, place, vocab = call(
        request_kernel,
        (
            jax.ShapeDtypeStruct((groups, HALF), jnp.int32),
            jax.ShapeDtypeStruct((1, doc_slots), jnp.int32),
            jax.ShapeDtypeStruct(vocab_table.shape[::-1], vocab_table.dtype),
        ),
        [SMEM, VMEM, VMEM, pl.BlockSpec(memory_space=pltpu.HBM)],
        [pltpu.SemaphoreType.DMA],
        limit=48,
    )(core, word_shard.reshape(1, slots), word_row, vocab_table.T)
    asked = swap(requests.reshape(groups, 1, HALF), "docs")
    own_atoms = support_atoms.T
    other_atoms = lax.ppermute(own_atoms, "supp", pairs)
    own_logits = weight_logits.reshape(1, atoms)
    other_logits = lax.ppermute(own_logits, "supp", pairs)
    found = call(
        lookup_kernel,
        jax.ShapeDtypeStruct((groups * HALF, TILES * LANES), jnp.bfloat16),
        [SMEM, VMEM],
        [
            pltpu.VMEM(((vocab_table.shape[0] + 8) // 8 * 8 * TILES, LANES), jnp.float32),
            pltpu.VMEM((groups * HALF * TILES + 8, LANES), jnp.float32),
        ],
        limit=24,
    )(asked, vocab)
    own = swap(found.reshape(groups, HALF, TILES * LANES), "docs")
    own = own.reshape(groups * HALF, TILES * LANES)
    own, other_logits = lax.optimization_barrier((own, other_logits))
    other = lax.ppermute(own, "supp", pairs)

    plan, extent, peak, start = call(
        first_kernel,
        (
            jax.ShapeDtypeStruct((doc_slots, 2 * atoms), jnp.bfloat16),
            f32((parts // 2, 1, doc_slots + LANES)),
            f32((1, doc_slots)),
            f32((1, 2 * atoms)),
        ),
        [SMEM, SMEM] + [VMEM] * 7,
        [
            pltpu.VMEM((doc_slots, 2 * groups * HALF), jnp.bfloat16),
            pltpu.VMEM((doc_slots, width), jnp.bfloat16),
            pltpu.VMEM((doc_slots, LANES), jnp.float32),
            pltpu.VMEM((doc_slots, 2 * atoms), jnp.float32),
            pltpu.VMEM((doc_slots, LANES), jnp.float32),
            pltpu.VMEM((8, 2 * atoms), jnp.float32),
            pltpu.VMEM((doc_slots, LANES), jnp.float32),
            pltpu.VMEM((doc_slots, LANES), jnp.float32),
        ],
        limit=32,
    )(core, word_counts, own, other, place, own_atoms, other_atoms, own_logits, other_logits)
    extents = swap(extent, "supp", same_core)
    mass, scale, base, gain, own_col, other_col = call(
        second_kernel,
        (
            f32((parts // 2, 1, doc_slots)),
            f32((1, doc_slots)),
            f32((1, doc_slots)),
            f32((1, 2 * atoms)),
            f32((1, atoms)),
            f32((1, atoms)),
        ),
        [SMEM, SMEM] + [VMEM] * 6,
        limit=12,
    )(core, word_counts, extents, peak, plan, start, own_logits, other_logits)
    masses = swap(mass, "supp", same_core)
    marginal, passed = call(
        third_kernel,
        (f32((2 * groups, 1, atoms)), f32((1, doc_slots + atoms))),
        [SMEM, SMEM] + [VMEM] * 6,
        limit=12,
    )(core, word_counts, masses, scale, base, plan, gain, other_col)
    marginals = swap(marginal, ("docs", "supp"), same_level)
    back = lax.ppermute(passed, "supp", pairs)
    mean, part = call(
        lambda *refs: mean_kernel(docs * groups, *refs),
        (f32((1, atoms)), f32((parts, 1, LANES))),
        [VMEM],
        limit=8,
    )(marginals)
    shares = swap(part, "supp")
    row_pot, col_pot = call(
        output_kernel,
        (f32((docs, doc_slots)), f32((docs, atoms))),
        [SMEM] + [VMEM] * 4,
        limit=8,
    )(core, passed, back, own_col, own_atoms)
    new_log = call(final_kernel, f32((1, atoms)), [VMEM, VMEM], limit=8)(shares, mean)
    return row_pot, col_pot, new_log.reshape(atoms)


def solution(mesh):
    placed = (P("docs", None), P("supp", None), P("supp"), P("docs"), P("docs", None), P("docs"))
    return jax.shard_map(
        shards,
        mesh=mesh,
        in_specs=placed,
        out_specs=(P("docs", None), P("docs", "supp"), P("supp")),
        check_vma=False,
    )
```
